1024 devices in a mesh: seq: 64 (over y, x), head: 16 (over z, core).
Axes of the slice: x: 8, y: 8, z: 8, core: 2. Of those that a mesh axis runs over, the one named last changes fastest.
Arguments:
- queries: bfloat16 [8192, 4096], P('seq', 'head'), may hold values from -64 to 64
- keys: bfloat16 [8192, 4096], P('seq', 'head'), may hold values from -8 to 8
- values: bfloat16 [8192, 4096], P('seq', 'head'), may hold values from -8 to 8
- gate: float32 [32], P('head'), may hold values from -6 to 6
- out_weight: bfloat16 [4096, 4096], P('head'), may hold values from -0.09375 to 0.09375
- out_grad: bfloat16 [8192, 4096], P('seq', 'head'), may hold values from -6 to 6
- valid: int32 [64], P('seq'), may hold values from 32 to 128, as said below
- starts: int32 [64], P('seq'), may hold values from 0 to 1, as said below
Outputs:
- output: bfloat16 [8192, 4096], P('seq', 'head')
- query_grad: bfloat16 [8192, 4096], P('seq', 'head')
- key_grad: bfloat16 [8192, 4096], P('seq', 'head')
- value_grad: bfloat16 [8192, 4096], P('seq', 'head')
The draws below stay inside these ranges and needn't reach their ends.
Inputs may be any that keep to these rules, and one draw needn't show every extreme that they name: `valid`: A segment with fewer than 128 live tokens is followed by a segment that starts a document, or is the last one. The first segment starts a document and the second does not.
All inputs are finite; a program needn't handle non-finite values.
Results may differ from the reference program's by a relative error of at most 0.029.
Values may be sent and summed in bfloat16 or wider, within the bound.
A program may use at most 64 MiB of HBM per device.

```python
import jax
import jax.numpy as jnp
from jax import lax

H = 32
DH = 128
D = 4096
TOK_DEV = 128
NSEG = 64
TOKENS = 8192


def streams(key):
    base_key = jax.random.fold_in(key, 101)
    keys_list = jax.random.split(base_key, 5)
    segs = TOKENS // TOK_DEV
    width = H * DH

    def noise(sub_key, shape):
        return jax.random.truncated_normal(sub_key, -4.0, 4.0, shape, jnp.float32)
    key_offset = jnp.repeat(noise(keys_list[1], (segs, width)), TOK_DEV, axis=0)
    value_offset = jnp.repeat(noise(keys_list[3], (segs, width)), TOK_DEV, axis=0)
    key_drawn = 0.8 * noise(keys_list[0], (TOKENS, width)) + 0.6 * key_offset
    value_vals = 0.8 * noise(keys_list[2], (TOKENS, width)) + 0.8 * value_offset
    query_vals = noise(keys_list[4], (TOKENS, width))
    key_vals = key_drawn
    return (query_vals, key_vals, value_vals)


def draw_queries(key, part):
    return streams(key)[0].astype(jnp.bfloat16)


def draw_keys(key, part):
    return streams(key)[1].astype(jnp.bfloat16)


def draw_values(key, part):
    return streams(key)[2].astype(jnp.bfloat16)


def documents(key):
    split_keys = jax.random.split(jax.random.fold_in(key, 202), 3)
    index = jnp.arange(NSEG)
    coin = (jax.random.randint(split_keys[0], (NSEG,), 0, 6) == 0).astype(jnp.int32)
    forced = jax.random.randint(split_keys[2], (), 2, NSEG)
    coin = jnp.where(index == forced, 1, coin)
    starts = jnp.where(index == 0, 1, jnp.where(index == 1, 0, coin)).astype(jnp.int32)
    following = jnp.concatenate([starts[1:], jnp.ones((1,), jnp.int32)])
    short = jax.random.randint(split_keys[1], (NSEG,), TOK_DEV // 4, TOK_DEV)
    short = jnp.where(index == NSEG - 1, TOK_DEV // 4, short)
    valid = jnp.where(following == 1, short, TOK_DEV).astype(jnp.int32)
    return (valid, starts)


def draw_valid(key, part):
    return documents(key)[0]


def draw_starts(key, part):
    return documents(key)[1]


def block_scale(own_key, dims, pieces, least, top_value):
    def one(dim, blocks):
        steps = jax.random.uniform(jax.random.fold_in(jax.random.fold_in(own_key, 6), dim), (blocks,), jnp.float32, least / len(pieces), top_value / len(pieces))
        return jnp.repeat(jnp.exp(steps), dims[dim] // blocks).reshape((-1,) + (1,) * (len(dims) - dim - 1))

    factor_of = one(*pieces[0])
    for cut in pieces[1:]:
        factor_of = factor_of * one(*cut)
    return factor_of


def gaussian(rng, dims, scale, limit, cuts=(), held_as=jnp.bfloat16):
    gain = block_scale(rng, dims, cuts, -0.22, 0.18) if cuts else 1.0
    values = jax.random.normal(rng, dims, jnp.float32) * scale * gain
    return jnp.minimum(jnp.maximum(values, -limit), limit).astype(held_as)


def setup_inputs(seed: int = 0) -> dict:
    splits = jax.random.split(jax.random.key(seed), 9)
    queries = draw_queries(jax.random.fold_in(splits[8], 71), 0)
    keys = draw_keys(jax.random.fold_in(splits[8], 71), 0)
    values = draw_values(jax.random.fold_in(splits[8], 71), 0)
    gate = gaussian(splits[3], (H,), 2.0, 6.0, ((0, 16),), jnp.float32)
    out_weight = gaussian(splits[4], (H * DH, D), D ** -0.5, 0.09375, ((0, 16),))
    out_grad = gaussian(splits[5], (TOKENS, D), 1.0, 6.0, ((0, 64), (1, 16)))
    valid = draw_valid(jax.random.fold_in(splits[8], 71), 0)
    starts = draw_starts(jax.random.fold_in(splits[8], 71), 0)
    return {"queries": queries, "keys": keys, "values": values, "gate": gate, "out_weight": out_weight, "out_grad": out_grad, "valid": valid, "starts": starts}


precise = lax.Precision.HIGHEST

def feature_map(inputs):
    return jnp.where(inputs > 0, inputs + 1.0, jnp.exp(jnp.minimum(inputs, 0.0)))

def segment_state(key_vals, value_vals, live_mask):
    length = key_vals.shape[0]
    sig_keys = feature_map(key_vals.reshape(length, -1, DH)) * live_mask[:, None, None]
    val_heads = value_vals.reshape(length, -1, DH) * live_mask[:, None, None]
    memory = jnp.einsum('thd,the->hde', sig_keys, val_heads, precision=precise)
    return (memory, lax.optimization_barrier(jnp.sum(sig_keys, axis=0)))

def segment_read(query_vals, key_vals, value_vals, live_mask, memory, norm_sum, gate_weight):
    length = query_vals.shape[0]
    query_heads = query_vals.reshape(length, -1, DH)
    query_low = query_heads.astype(jnp.bfloat16)
    key_low = key_vals.reshape(length, -1, DH).astype(jnp.bfloat16)
    value_low = value_vals.reshape(length, -1, DH).astype(jnp.bfloat16)
    sig_query = feature_map(query_heads)
    numer = jnp.einsum('thd,hde->the', sig_query, memory, precision=precise)
    denom = jnp.einsum('thd,hd->th', sig_query, norm_sum, precision=precise) + 1.0
    memory_read = numer / denom[:, :, None]
    scores = jnp.einsum('thd,shd->hts', query_low, key_low, preferred_element_type=jnp.float32) * DH ** (-0.5)
    where_pos = jnp.arange(length)
    allowed = (where_pos[None, :] <= where_pos[:, None]) & (live_mask[None, :] > 0)
    scores = jnp.where(allowed[None], scores, -1e+30)
    row_top = lax.stop_gradient(lax.optimization_barrier(jnp.max(scores, axis=-1, keepdims=True)))
    expo = jnp.exp(scores - row_top)
    probs = expo / lax.optimization_barrier(jnp.sum(expo, axis=-1, keepdims=True))
    probs_low = probs.astype(jnp.bfloat16)
    local_read = jnp.einsum('hts,she->the', probs_low, value_low, preferred_element_type=jnp.float32)
    mixed = gate_weight[None, :, None] * memory_read + (1.0 - gate_weight)[None, :, None] * local_read
    return (mixed * live_mask[:, None, None]).reshape(length, -1)

def reference(queries, keys, values, gate, out_weight, out_grad, valid, starts):
    segs = valid.shape[0]
    length = queries.shape[0] // segs

    def split_rows(array):
        return array.reshape(segs, length, array.shape[1])
    query_all = split_rows(queries.astype(jnp.float32))
    key_all = split_rows(keys.astype(jnp.float32))
    value_all = split_rows(values.astype(jnp.float32))
    live = (jnp.arange(length)[None, :] < valid[:, None]).astype(jnp.float32)
    opened = (1 - starts).astype(jnp.float32)
    gate_weight = jax.nn.sigmoid(gate)

    def state_one(item):
        return segment_state(item[0], item[1], item[2])
    memory_local, norm_local = lax.map(state_one, (key_all, value_all, live))
    zero_state = (jnp.zeros(memory_local.shape[1:], jnp.float32), jnp.zeros(norm_local.shape[1:], jnp.float32))

    def forward_step(carry, item):
        memory_used = item[2] * carry[0]
        norm_used = item[2] * carry[1]
        return ((memory_used + item[0], norm_used + item[1]), (memory_used, norm_used))
    _, (memory_in, norm_in) = lax.scan(forward_step, zero_state, (memory_local, norm_local, opened))

    def read_one(item):
        return segment_read(item[0], item[1], item[2], item[3], item[4], item[5], gate_weight).astype(jnp.bfloat16)
    mixed = lax.map(read_one, (query_all, key_all, value_all, live, memory_in, norm_in)).reshape(-1, out_weight.shape[0])
    output = jnp.dot(mixed, out_weight, preferred_element_type=jnp.float32).astype(jnp.bfloat16)
    mixed_grad = jnp.dot(out_grad, out_weight.T, preferred_element_type=jnp.float32).astype(jnp.bfloat16)
    mixed_grad = lax.optimization_barrier(mixed_grad).astype(jnp.float32)
    mixed_grad = split_rows(mixed_grad)

    def backward_one(item):
        live_mask = item[3]

        def read_local(query_arg, key_arg, value_arg, memory_arg, norm_arg):
            return segment_read(query_arg, key_arg, value_arg, live_mask, memory_arg, norm_arg, gate_weight)
        _, pullback = jax.vjp(read_local, item[0], item[1], item[2], item[4], item[5])
        return pullback(item[6])
    query_part, key_part, value_part, memory_grad, norm_grad = lax.map(backward_one, (query_all, key_all, value_all, live, memory_in, norm_in, mixed_grad))

    def reverse_step(carry, item):
        passed = (item[2] * (item[0] + carry[0]), item[2] * (item[1] + carry[1]))
        return (passed, carry)
    _, (memory_back, norm_back) = lax.scan(reverse_step, zero_state, (memory_grad, norm_grad, opened), reverse=True)

    def state_back(item):
        live_mask = item[2]

        def state_local(key_arg, value_arg):
            return segment_state(key_arg, value_arg, live_mask)
        _, pullback = jax.vjp(state_local, item[0], item[1])
        return pullback((item[3], item[4]))
    key_more, value_more = lax.map(state_back, (key_all, value_all, live, memory_back, norm_back))
    width = queries.shape[1]
    query_grad = query_part.reshape(-1, width).astype(jnp.bfloat16)
    key_grad = (key_part + key_more).reshape(-1, width).astype(jnp.bfloat16)
    value_grad = (value_part + value_more).reshape(-1, width).astype(jnp.bfloat16)
    return (output, query_grad, key_grad, value_grad)
```

```python
import functools

import jax
import jax.numpy as jnp
from jax import lax
from jax.experimental import pallas as pl
from jax.experimental.pallas import tpu as pltpu
from jax.sharding import PartitionSpec as P

DH = 128
LENGTH = 128
WIDTH = 2 * DH
SMALL = 16
SCALE = DH ** (-0.5)
MESH = pl.DeviceIdType.MESH
F32, BF16 = jnp.float32, jnp.bfloat16


def dot(a, b, contract_a, contract_b):
    return lax.dot_general(
        a, b, (((contract_a,), (contract_b,)), ((), ())), preferred_element_type=F32
    )


def phi(x):
    return jnp.where(x > 0, x + 1.0, jnp.exp(jnp.minimum(x, 0.0)))


def phi_slope(x):
    return jnp.where(x > 0, 1.0, jnp.where(x == 0, 0.5, jnp.exp(jnp.minimum(x, 0.0))))


def both(one):
    return jnp.concatenate([one(slice(0, DH)), one(slice(DH, WIDTH))], axis=1)


def small_rows(norm, flag):
    high = norm.astype(BF16).astype(F32)
    at = lax.broadcasted_iota(jnp.int32, (SMALL, WIDTH), 0)
    rows = jnp.where(at == 0, high, jnp.where(at == 1, norm - high, jnp.where(at == 2, flag, 0.0)))
    return rows.astype(BF16)


def split_small(ref, place, rows):
    small = ref[place, rows : rows + SMALL, :].astype(F32)
    return small[0:1] + small[1:2], small[2:3]


class Scan:
    def __init__(self, me, sizes, reverse, msg1, buf1, msg2, buf2, msg3, carried, send, recv):
        self.me, self.sizes, self.reverse = me, sizes, reverse
        self.msg1, self.buf1, self.msg2, self.buf2 = msg1, buf1, msg2, buf2
        self.msg3, self.carried, self.send, self.recv = msg3, carried, send, recv
        self.rows = LENGTH // sizes[0]
        self.sent = []

    def copy(self, phase, j, src, dst, peer):
        one = pltpu.make_async_remote_copy(
            src_ref=src,
            dst_ref=dst,
            send_sem=self.send.at[phase, j],
            recv_sem=self.recv.at[phase, j],
            device_id=peer,
            device_id_type=MESH,
        )
        one.start()
        self.sent.append(one)
        return one

    def start(self, state, norm, flag):
        x = self.me["x"]
        small = small_rows(norm, flag)
        state = state.astype(BF16)
        for i in range(self.sizes[0]):
            self.msg1[i, 0 : self.rows, :] = state[i * self.rows : (i + 1) * self.rows]
            self.msg1[i, self.rows :, :] = small
        self.buf1[x] = self.msg1[x]

    def send_first(self):
        x, X = self.me["x"], self.sizes[0]
        self.first = []
        for j in range(1, X):
            to = lax.rem(x + j, X)
            self.first.append(
                self.copy(0, j, self.msg1.at[to], self.buf1.at[x], self.me["x_peer"](j))
            )

    def step(self, i, carry):
        acc, acc_norm, still_open = carry
        norm, flag = split_small(self.buf1, i, self.rows)
        block = self.buf1[i, 0 : self.rows, :].astype(F32)
        opened = 1.0 - flag
        if self.reverse:
            return acc, acc_norm, (
                opened * (acc + block),
                opened * (acc_norm + norm),
                still_open * opened,
            )
        acc, acc_norm = opened * acc, opened * acc_norm
        return acc, acc_norm, (acc + block, acc_norm + norm, still_open * opened)

    def order(self, n):
        return range(n - 1, -1, -1) if self.reverse else range(n)

    def second(self):
        for one in self.first:
            one.wait_recv()
        y, (X, Y) = self.me["y"], self.sizes
        carry = (
            jnp.zeros((self.rows, WIDTH), F32),
            jnp.zeros((1, WIDTH), F32),
            jnp.ones((1, WIDTH), F32),
        )
        for i in self.order(X):
            _, _, carry = self.step(i, carry)
        self.msg2[0 : self.rows, :] = carry[0].astype(BF16)
        self.msg2[self.rows :, :] = small_rows(carry[1], carry[2])
        self.buf2[y] = self.msg2[...]
        self.waits = [
            self.copy(1, j, self.msg2, self.buf2.at[y], self.me["y_peer"](j)) for j in range(1, Y)
        ]

    def third(self):
        for one in self.waits:
            one.wait_recv()
        x, y, (X, Y) = self.me["x"], self.me["y"], self.sizes
        acc, acc_norm = jnp.zeros((self.rows, WIDTH), F32), jnp.zeros((1, WIDTH), F32)
        at = jnp.full((1, WIDTH), y, jnp.int32)
        for i in self.order(Y):
            norm, still_open = split_small(self.buf2, i, self.rows)
            block = self.buf2[i, 0 : self.rows, :].astype(F32)
            counts = jnp.where((at < i) if self.reverse else (at > i), 1.0, 0.0)
            acc = counts * (block + still_open * acc) + (1.0 - counts) * acc
            acc_norm = counts * (norm + still_open * acc_norm) + (1.0 - counts) * acc_norm
        carry = (acc, acc_norm, jnp.ones((1, WIDTH), F32))
        mine = jnp.zeros((1, WIDTH), F32)
        at = jnp.full((1, WIDTH), x, jnp.int32)
        for i in self.order(X):
            enters, enters_norm, carry = self.step(i, carry)
            self.msg3[i] = enters.astype(BF16)
            mine = jnp.where(at == i, enters_norm, mine)
        here = pl.ds(pl.multiple_of(x * self.rows, self.rows), self.rows)
        self.carried[here, :] = self.msg3[x]
        self.waits = []
        for j in range(1, X):
            to = lax.rem(x + j, X)
            self.waits.append(
                self.copy(2, j, self.msg3.at[to], self.carried.at[here, :], self.me["x_peer"](j))
            )
        return mine

    def finish(self):
        for one in self.waits:
            one.wait_recv()
        return self.carried[...]


def layer(
    sizes,
    gate_ref,
    valid_ref,
    starts_ref,
    q_hbm,
    k_hbm,
    v_hbm,
    og_hbm,
    w_hbm,
    out_hbm,
    dq_hbm,
    dk_hbm,
    dv_hbm,
    q_ref,
    k_ref,
    v_ref,
    og_all,
    w_ref,
    w_other,
    results,
    probs_ref,
    local_ref,
    sigq_ref,
    read_ref,
    mixed_ref,
    mixed_other,
    rs_send,
    rs_recv,
    f_msg1,
    f_buf1,
    f_msg2,
    f_buf2,
    f_msg3,
    f_in,
    b_msg1,
    b_buf1,
    b_msg2,
    b_buf2,
    b_msg3,
    b_in,
    load_sem,
    store_sem,
    f_send,
    f_recv,
    b_send,
    b_recv,
    ag_send,
    ag_recv,
    fw_send,
    fw_recv,
    w_send,
    w_recv,
    mix_send,
    mix_recv,
    r_send,
    r_recv,
):
    X, Y, Z = sizes
    seq, head = lax.axis_index("seq"), lax.axis_index("head")
    y, x = lax.div(seq, X), lax.rem(seq, X)
    z, core = lax.div(head, 2), lax.rem(head, 2)

    def x_peer(j):
        return (y * X + lax.rem(x + j, X), head)

    def y_peer(j):
        return (lax.rem(y + j, Y) * X + x, head)

    def z_peer(j):
        return (seq, lax.rem(z + j, Z) * 2 + core)

    partner = (seq, z * 2 + (1 - core))
    me = {"x": x, "y": y, "x_peer": x_peer, "y_peer": y_peer}
    sent = []

    def remote(src, dst, send, recv, peer):
        one = pltpu.make_async_remote_copy(
            src_ref=src,
            dst_ref=dst,
            send_sem=send,
            recv_sem=recv,
            device_id=peer,
            device_id_type=MESH,
        )
        one.start()
        sent.append(one)
        return one

    loads = {}
    for n, (name, src, dst) in enumerate(
        (
            ("k", k_hbm, k_ref),
            ("v", v_hbm, v_ref),
            ("og", og_hbm, og_all.at[head]),
            ("q", q_hbm, q_ref),
            ("w", w_hbm, w_ref),
        )
    ):
        loads[name] = pltpu.make_async_copy(src, dst, load_sem.at[n])
        loads[name].start()

    barrier = pltpu.get_barrier_semaphore()
    peers = [x_peer(j) for j in range(1, X)] + [y_peer(j) for j in range(1, Y)]
    peers += [z_peer(j) for j in range(1, Z)] + [partner]
    for peer in peers:
        pl.semaphore_signal(barrier, inc=1, device_id=peer, device_id_type=MESH)

    forward = Scan(
        me, (X, Y), False, f_msg1, f_buf1, f_msg2, f_buf2, f_msg3, f_in, f_send, f_recv
    )
    backward = Scan(
        me, (X, Y), True, b_msg1, b_buf1, b_msg2, b_buf2, b_msg3, b_in, b_send, b_recv
    )

    live = lax.broadcasted_iota(jnp.int32, (LENGTH, WIDTH), 0) < valid_ref[0]
    flag = jnp.full((1, WIDTH), starts_ref[0], jnp.int32).astype(F32)
    lanes = lax.broadcasted_iota(jnp.int32, (1, WIDTH), 1)
    logit = jnp.where(
        lanes < DH, jnp.full((1, WIDTH), gate_ref[0], F32), jnp.full((1, WIDTH), gate_ref[1], F32)
    )
    gate = 1.0 / (1.0 + jnp.exp(-logit))

    loads["k"].wait()
    loads["v"].wait()
    sigk = jnp.where(live, phi(k_ref[...].astype(F32)), 0.0)
    sigk_low = sigk.astype(BF16)
    v_low = v_ref[...]
    state = both(lambda h: dot(sigk_low[:, h], v_low[:, h], 0, 0))
    forward.start(state, jnp.sum(sigk, axis=0, keepdims=True), flag)

    pl.semaphore_wait(barrier, len(peers))
    forward.send_first()

    loads["og"].wait()
    gathers = [
        remote(og_all.at[head], og_all.at[head], ag_send.at[j], ag_recv.at[j], z_peer(j))
        for j in range(1, Z)
    ]
    passed = [remote(og_all.at[head], og_all.at[head], fw_send.at[0], fw_recv.at[0], partner)]
    weights = []
    for i in range(Z):
        columns = pl.ds(pl.multiple_of((2 * i + 1 - core) * WIDTH, WIDTH), WIDTH)
        weights.append(
            remote(w_hbm.at[:, columns], w_other.at[i], w_send.at[i], w_recv.at[i], partner)
        )

    loads["q"].wait()
    row = lax.broadcasted_iota(jnp.int32, (LENGTH, LENGTH), 0)
    col = lax.broadcasted_iota(jnp.int32, (LENGTH, LENGTH), 1)
    allowed = (col <= row) & (col < valid_ref[0])
    for n in range(2):
        h = slice(n * DH, (n + 1) * DH)
        scores = dot(q_ref[:, h], k_ref[:, h], 1, 1) * SCALE
        scores = jnp.where(allowed, scores, -1e30)
        expo = jnp.exp(scores - jnp.max(scores, axis=1, keepdims=True))
        probs = expo / jnp.sum(expo, axis=1, keepdims=True)
        probs_ref[n] = probs
        local_ref[:, h] = dot(probs.astype(BF16), v_ref[:, h], 1, 0)

    forward.second()
    sigq = phi(q_ref[...].astype(F32))
    sigq_ref[...] = sigq.astype(BF16)
    norm_in = forward.third()

    def pass_on(j):
        gathers[j - 1].wait_recv()
        block = og_all.at[lax.rem(z - j + Z, Z) * 2 + core]
        passed.append(remote(block, block, fw_send.at[j], fw_recv.at[j], partner))

    scaled = sigq * norm_in
    inverse = both(
        lambda h: jnp.broadcast_to(
            1.0 / (jnp.sum(scaled[:, h], axis=1, keepdims=True) + 1.0), (LENGTH, DH)
        )
    )

    mem_in = forward.finish()
    read = both(lambda h: dot(sigq_ref[:, h], mem_in[:, h], 1, 0)) * inverse
    read_ref[...] = read
    mixed = jnp.where(live, gate * read + (1.0 - gate) * local_ref[...], 0.0)
    mixed_ref[...] = mixed.astype(BF16)
    mixing = remote(mixed_ref, mixed_other, mix_send.at[0], mix_recv.at[0], partner)

    near_first = sorted(range(1, Z), key=lambda j: min(j, Z - j))
    for j in near_first:
        pass_on(j)

    loads["w"].wait()
    for one in weights:
        one.wait_recv()
    mixing.wait_recv()

    def part(target):
        columns = pl.ds(pl.multiple_of((2 * target + core) * WIDTH, WIDTH), WIDTH)
        return dot(mixed_ref[...], w_ref[:, columns], 1, 0) + dot(
            mixed_other[...], w_other[target], 1, 0
        )

    reduces = []
    for j in reversed(near_first):
        rs_send[j] = part(lax.rem(z + j, Z)).astype(BF16)
        reduces.append(
            remote(rs_send.at[j], rs_recv.at[j], r_send.at[j], r_recv.at[j], z_peer(j))
        )

    for one in passed:
        one.wait_recv()
    grad = jnp.zeros((LENGTH, WIDTH), F32)
    for i in range(2 * Z):
        grad = grad + dot(og_all[i], w_ref[:, i * WIDTH : (i + 1) * WIDTH], 1, 1)
    grad = jnp.where(live, grad.astype(BF16).astype(F32), 0.0)
    read_grad = gate * grad
    local_grad = ((1.0 - gate) * grad).astype(BF16)
    numer_grad = (read_grad * inverse).astype(BF16)
    product = read_grad * read_ref[...]
    denom_grad = -inverse * both(
        lambda h: jnp.broadcast_to(jnp.sum(product[:, h], axis=1, keepdims=True), (LENGTH, DH))
    )
    state_grad = both(lambda h: dot(sigq_ref[:, h], numer_grad[:, h], 0, 0))
    norm_grad = jnp.sum(phi(q_ref[...].astype(F32)) * denom_grad, axis=0, keepdims=True)
    backward.start(state_grad, norm_grad, flag)
    backward.send_first()

    parts = []
    for n in range(2):
        h = slice(n * DH, (n + 1) * DH)
        probs = probs_ref[n]
        probs_grad = dot(local_grad[:, h], v_ref[:, h], 1, 1)
        inner = jnp.sum(probs_grad * probs, axis=1, keepdims=True)
        scores_grad = (probs * (probs_grad - inner) * SCALE).astype(BF16)
        parts.append(
            (
                dot(scores_grad, k_ref[:, h], 1, 0)
                + (dot(numer_grad[:, h], f_in[:, h], 1, 1) + denom_grad[:, h] * norm_in[:, h])
                * phi_slope(q_ref[:, h].astype(F32)),
                dot(scores_grad, q_ref[:, h], 0, 0),
                dot(probs.astype(BF16), local_grad[:, h], 0, 0),
            )
        )
    stores = []

    def store(n, value, target):
        results[n] = value.astype(BF16)
        one = pltpu.make_async_copy(results.at[n], target, store_sem.at[n])
        one.start()
        stores.append(one)

    store(1, jnp.concatenate([parts[0][0], parts[1][0]], axis=1), dq_hbm)
    key_part = jnp.concatenate([parts[0][1], parts[1][1]], axis=1)
    value_part = jnp.concatenate([parts[0][2], parts[1][2]], axis=1)
    own = part(z)

    backward.second()
    norm_back = backward.third()
    mem_back = backward.finish()
    k_float = k_ref[...].astype(F32)
    key_more = (both(lambda h: dot(v_ref[:, h], mem_back[:, h], 1, 1)) + norm_back) * phi_slope(
        k_float
    )
    store(2, key_part + jnp.where(live, key_more, 0.0), dk_hbm)
    sigk_low = jnp.where(live, phi(k_float), 0.0).astype(BF16)
    store(3, value_part + both(lambda h: dot(sigk_low[:, h], mem_back[:, h], 1, 0)), dv_hbm)

    total = own
    for j, one in zip(reversed(near_first), reduces):
        one.wait_recv()
        total = total + rs_recv[j].astype(F32)
    store(0, total, out_hbm)

    for one in sent + forward.sent + backward.sent:
        one.wait_send()
    for one in stores:
        one.wait()


def build(mesh, X):
    Y, Z = mesh.shape["seq"] // X, mesh.shape["head"] // 2
    rows = LENGTH // X
    dma = pltpu.SemaphoreType.DMA

    def scan_scratch():
        return [
            pltpu.VMEM((X, rows + SMALL, WIDTH), BF16),
            pltpu.VMEM((X, rows + SMALL, WIDTH), BF16),
            pltpu.VMEM((rows + SMALL, WIDTH), BF16),
            pltpu.VMEM((Y, rows + SMALL, WIDTH), BF16),
            pltpu.VMEM((X, rows, WIDTH), BF16),
            pltpu.VMEM((LENGTH, WIDTH), BF16),
        ]

    def block():
        return pltpu.VMEM((LENGTH, WIDTH), BF16)

    def wide():
        return pltpu.VMEM((LENGTH, WIDTH), F32)

    most = max(X, Y)
    scratch = [
        block(),
        block(),
        block(),
        pltpu.VMEM((2 * Z, LENGTH, WIDTH), BF16),
        pltpu.VMEM((WIDTH, 2 * Z * WIDTH), BF16),
        pltpu.VMEM((Z, WIDTH, WIDTH), BF16),
        pltpu.VMEM((4, LENGTH, WIDTH), BF16),
        pltpu.VMEM((2, LENGTH, LENGTH), F32),
        wide(),
        block(),
        wide(),
        block(),
        block(),
        pltpu.VMEM((Z, LENGTH, WIDTH), BF16),
        pltpu.VMEM((Z, LENGTH, WIDTH), BF16),
        *scan_scratch(),
        *scan_scratch(),
        dma((5,)),
        dma((4,)),
        dma((3, most)),
        dma((3, most)),
        dma((3, most)),
        dma((3, most)),
        dma((Z,)),
        dma((Z,)),
        dma((Z,)),
        dma((Z,)),
        dma((Z,)),
        dma((Z,)),
        dma((1,)),
        dma((1,)),
        dma((Z,)),
        dma((Z,)),
    ]

    def shards(queries, keys, values, gate, out_weight, out_grad, valid, starts):
        one = jax.ShapeDtypeStruct((LENGTH, WIDTH), BF16)
        return pl.pallas_call(
            functools.partial(layer, (X, Y, Z)),
            out_shape=(one,) * 4,
            in_specs=[pl.BlockSpec(memory_space=pltpu.SMEM)] * 3
            + [pl.BlockSpec(memory_space=pl.ANY)] * 5,
            out_specs=(pl.BlockSpec(memory_space=pl.ANY),) * 4,
            scratch_shapes=scratch,
            compiler_params=pltpu.CompilerParams(
                collective_id=0, has_side_effects=True, vmem_limit_bytes=40 * 1024 * 1024
            ),
            name="layer",
        )(gate, valid, starts, queries, keys, values, out_grad, out_weight)

    placed = (
        P("seq", "head"),
        P("seq", "head"),
        P("seq", "head"),
        P("head"),
        P("head", None),
        P("seq", "head"),
        P("seq"),
        P("seq"),
    )
    return jax.shard_map(
        shards, mesh=mesh, in_specs=placed, out_specs=(P("seq", "head"),) * 4, check_vma=False
    )


def solution(mesh):
    return build(mesh, 8)
```

```python
import functools

import jax
import jax.numpy as jnp
from jax import lax
from jax.experimental import pallas as pl
from jax.experimental.pallas import tpu as pltpu
from jax.sharding import PartitionSpec as P

DH = 128
LENGTH = 128
WIDTH = 2 * DH
SMALL = 16
SCALE = DH ** (-0.5)
MESH = pl.DeviceIdType.MESH
F32, BF16 = jnp.float32, jnp.bfloat16


def dot(a, b, contract_a, contract_b):
    return lax.dot_general(
        a, b, (((contract_a,), (contract_b,)), ((), ())), preferred_element_type=F32
    )


def phi(x):
    return jnp.where(x > 0, x + 1.0, jnp.exp(jnp.minimum(x, 0.0)))


def phi_slope(x):
    return jnp.where(x > 0, 1.0, jnp.where(x == 0, 0.5, jnp.exp(jnp.minimum(x, 0.0))))


def both(one):
    return jnp.concatenate([one(slice(0, DH)), one(slice(DH, WIDTH))], axis=1)


def small_rows(norm, flag):
    high = norm.astype(BF16).astype(F32)
    at = lax.broadcasted_iota(jnp.int32, (SMALL, WIDTH), 0)
    rows = jnp.where(at == 0, high, jnp.where(at == 1, norm - high, jnp.where(at == 2, flag, 0.0)))
    return rows.astype(BF16)


def split_small(ref, place, rows):
    small = ref[place, rows : rows + SMALL, :].astype(F32)
    return small[0:1] + small[1:2], small[2:3]


class Scan:
    def __init__(self, me, sizes, reverse, msg1, buf1, msg2, buf2, msg3, carried, send, recv):
        self.me, self.sizes, self.reverse = me, sizes, reverse
        self.msg1, self.buf1, self.msg2, self.buf2 = msg1, buf1, msg2, buf2
        self.msg3, self.carried, self.send, self.recv = msg3, carried, send, recv
        self.rows = LENGTH // sizes[0]
        self.sent = []

    def copy(self, phase, j, src, dst, peer):
        one = pltpu.make_async_remote_copy(
            src_ref=src,
            dst_ref=dst,
            send_sem=self.send.at[phase, j],
            recv_sem=self.recv.at[phase, j],
            device_id=peer,
            device_id_type=MESH,
        )
        one.start()
        self.sent.append(one)
        return one

    def start(self, state, norm, flag):
        x = self.me["x"]
        small = small_rows(norm, flag)
        state = state.astype(BF16)
        for i in range(self.sizes[0]):
            self.msg1[i, 0 : self.rows, :] = state[i * self.rows : (i + 1) * self.rows]
            self.msg1[i, self.rows :, :] = small
        self.buf1[x] = self.msg1[x]

    def send_first(self):
        x, X = self.me["x"], self.sizes[0]
        self.first = []
        for j in range(1, X):
            to = lax.rem(x + j, X)
            self.first.append(
                self.copy(0, j, self.msg1.at[to], self.buf1.at[x], self.me["x_peer"](j))
            )

    def step(self, i, carry):
        acc, acc_norm, still_open = carry
        norm, flag = split_small(self.buf1, i, self.rows)
        block = self.buf1[i, 0 : self.rows, :].astype(F32)
        opened = 1.0 - flag
        if self.reverse:
            return acc, acc_norm, (
                opened * (acc + block),
                opened * (acc_norm + norm),
                still_open * opened,
            )
        acc, acc_norm = opened * acc, opened * acc_norm
        return acc, acc_norm, (acc + block, acc_norm + norm, still_open * opened)

    def order(self, n):
        return range(n - 1, -1, -1) if self.reverse else range(n)

    def second(self):
        for one in self.first:
            one.wait_recv()
        y, (X, Y) = self.me["y"], self.sizes
        carry = (
            jnp.zeros((self.rows, WIDTH), F32),
            jnp.zeros((1, WIDTH), F32),
            jnp.ones((1, WIDTH), F32),
        )
        for i in self.order(X):
            _, _, carry = self.step(i, carry)
        self.msg2[0 : self.rows, :] = carry[0].astype(BF16)
        self.msg2[self.rows :, :] = small_rows(carry[1], carry[2])
        self.buf2[y] = self.msg2[...]
        self.waits = [
            self.copy(1, j, self.msg2, self.buf2.at[y], self.me["y_peer"](j)) for j in range(1, Y)
        ]

    def third(self):
        for one in self.waits:
            one.wait_recv()
        x, y, (X, Y) = self.me["x"], self.me["y"], self.sizes
        acc, acc_norm = jnp.zeros((self.rows, WIDTH), F32), jnp.zeros((1, WIDTH), F32)
        at = jnp.full((1, WIDTH), y, jnp.int32)
        for i in self.order(Y):
            norm, still_open = split_small(self.buf2, i, self.rows)
            block = self.buf2[i, 0 : self.rows, :].astype(F32)
            counts = jnp.where((at < i) if self.reverse else (at > i), 1.0, 0.0)
            acc = counts * (block + still_open * acc) + (1.0 - counts) * acc
            acc_norm = counts * (norm + still_open * acc_norm) + (1.0 - counts) * acc_norm
        carry = (acc, acc_norm, jnp.ones((1, WIDTH), F32))
        mine = jnp.zeros((1, WIDTH), F32)
        at = jnp.full((1, WIDTH), x, jnp.int32)
        for i in self.order(X):
            enters, enters_norm, carry = self.step(i, carry)
            self.msg3[i] = enters.astype(BF16)
            mine = jnp.where(at == i, enters_norm, mine)
        here = pl.ds(pl.multiple_of(x * self.rows, self.rows), self.rows)
        self.carried[here, :] = self.msg3[x]
        self.waits = []
        for j in range(1, X):
            to = lax.rem(x + j, X)
            self.waits.append(
                self.copy(2, j, self.msg3.at[to], self.carried.at[here, :], self.me["x_peer"](j))
            )
        return mine

    def finish(self):
        for one in self.waits:
            one.wait_recv()
        return self.carried[...]


def layer(
    sizes,
    gate_hbm,
    valid_hbm,
    starts_hbm,
    q_hbm,
    k_hbm,
    v_hbm,
    og_hbm,
    w_hbm,
    out_hbm,
    dq_hbm,
    dk_hbm,
    dv_hbm,
    gate_ref,
    valid_ref,
    starts_ref,
    q_ref,
    k_ref,
    v_ref,
    og_all,
    w_ref,
    w_other,
    results,
    probs_ref,
    local_ref,
    sigq_ref,
    read_ref,
    mixed_ref,
    mixed_other,
    rs_send,
    rs_recv,
    f_msg1,
    f_buf1,
    f_msg2,
    f_buf2,
    f_msg3,
    f_in,
    b_msg1,
    b_buf1,
    b_msg2,
    b_buf2,
    b_msg3,
    b_in,
    load_sem,
    store_sem,
    f_send,
    f_recv,
    b_send,
    b_recv,
    ag_send,
    ag_recv,
    fw_send,
    fw_recv,
    w_send,
    w_recv,
    mix_send,
    mix_recv,
    r_send,
    r_recv,
):
    X, Y, Z = sizes
    seq, head = lax.axis_index("seq"), lax.axis_index("head")
    y, x = lax.div(seq, X), lax.rem(seq, X)
    z, core = lax.div(head, 2), lax.rem(head, 2)

    def x_peer(j):
        return (y * X + lax.rem(x + j, X), head)

    def y_peer(j):
        return (lax.rem(y + j, Y) * X + x, head)

    def z_peer(j):
        return (seq, lax.rem(z + j, Z) * 2 + core)

    partner = (seq, z * 2 + (1 - core))
    me = {"x": x, "y": y, "x_peer": x_peer, "y_peer": y_peer}
    sent = []

    def remote(src, dst, send, recv, peer):
        one = pltpu.make_async_remote_copy(
            src_ref=src,
            dst_ref=dst,
            send_sem=send,
            recv_sem=recv,
            device_id=peer,
            device_id_type=MESH,
        )
        one.start()
        sent.append(one)
        return one

    loads = {}
    for n, (name, src, dst) in enumerate(
        (
            ("valid", valid_hbm, valid_ref),
            ("starts", starts_hbm, starts_ref),
            ("gate", gate_hbm, gate_ref),
            ("k", k_hbm, k_ref),
            ("v", v_hbm, v_ref),
            ("og", og_hbm, og_all.at[head]),
            ("q", q_hbm, q_ref),
            ("w", w_hbm, w_ref),
        )
    ):
        loads[name] = pltpu.make_async_copy(src, dst, load_sem.at[n])
        loads[name].start()

    barrier = pltpu.get_barrier_semaphore()
    peers = [x_peer(j) for j in range(1, X)] + [y_peer(j) for j in range(1, Y)]
    peers += [z_peer(j) for j in range(1, Z)] + [partner]
    for peer in peers:
        pl.semaphore_signal(barrier, inc=1, device_id=peer, device_id_type=MESH)

    forward = Scan(
        me, (X, Y), False, f_msg1, f_buf1, f_msg2, f_buf2, f_msg3, f_in, f_send, f_recv
    )
    backward = Scan(
        me, (X, Y), True, b_msg1, b_buf1, b_msg2, b_buf2, b_msg3, b_in, b_send, b_recv
    )

    for name in ("valid", "starts", "gate"):
        loads[name].wait()
    live = lax.broadcasted_iota(jnp.int32, (LENGTH, WIDTH), 0) < valid_ref[0]
    flag = jnp.full((1, WIDTH), starts_ref[0], jnp.int32).astype(F32)
    lanes = lax.broadcasted_iota(jnp.int32, (1, WIDTH), 1)
    logit = jnp.where(
        lanes < DH, jnp.full((1, WIDTH), gate_ref[0], F32), jnp.full((1, WIDTH), gate_ref[1], F32)
    )
    gate = 1.0 / (1.0 + jnp.exp(-logit))

    loads["k"].wait()
    loads["v"].wait()
    sigk = jnp.where(live, phi(k_ref[...].astype(F32)), 0.0)
    sigk_low = sigk.astype(BF16)
    v_low = v_ref[...]
    state = both(lambda h: dot(sigk_low[:, h], v_low[:, h], 0, 0))
    forward.start(state, jnp.sum(sigk, axis=0, keepdims=True), flag)

    pl.semaphore_wait(barrier, len(peers))
    forward.send_first()

    loads["og"].wait()
    gathers = [
        remote(og_all.at[head], og_all.at[head], ag_send.at[j], ag_recv.at[j], z_peer(j))
        for j in range(1, Z)
    ]
    passed = [remote(og_all.at[head], og_all.at[head], fw_send.at[0], fw_recv.at[0], partner)]
    weights = []
    for i in range(Z):
        columns = pl.ds(pl.multiple_of((2 * i + 1 - core) * WIDTH, WIDTH), WIDTH)
        weights.append(
            remote(w_hbm.at[:, columns], w_other.at[i], w_send.at[i], w_recv.at[i], partner)
        )

    loads["q"].wait()
    row = lax.broadcasted_iota(jnp.int32, (LENGTH, LENGTH), 0)
    col = lax.broadcasted_iota(jnp.int32, (LENGTH, LENGTH), 1)
    allowed = (col <= row) & (col < valid_ref[0])
    for n in range(2):
        h = slice(n * DH, (n + 1) * DH)
        scores = dot(q_ref[:, h], k_ref[:, h], 1, 1) * SCALE
        scores = jnp.where(allowed, scores, -1e30)
        expo = jnp.exp(scores - jnp.max(scores, axis=1, keepdims=True))
        probs = expo / jnp.sum(expo, axis=1, keepdims=True)
        probs_ref[n] = probs
        local_ref[:, h] = dot(probs.astype(BF16), v_ref[:, h], 1, 0)

    forward.second()
    sigq = phi(q_ref[...].astype(F32))
    sigq_ref[...] = sigq.astype(BF16)
    norm_in = forward.third()

    def pass_on(j):
        gathers[j - 1].wait_recv()
        block = og_all.at[lax.rem(z - j + Z, Z) * 2 + core]
        passed.append(remote(block, block, fw_send.at[j], fw_recv.at[j], partner))

    scaled = sigq * norm_in
    inverse = both(
        lambda h: jnp.broadcast_to(
            1.0 / (jnp.sum(scaled[:, h], axis=1, keepdims=True) + 1.0), (LENGTH, DH)
        )
    )

    mem_in = forward.finish()
    read = both(lambda h: dot(sigq_ref[:, h], mem_in[:, h], 1, 0)) * inverse
    read_ref[...] = read
    mixed = jnp.where(live, gate * read + (1.0 - gate) * local_ref[...], 0.0)
    mixed_ref[...] = mixed.astype(BF16)
    mixing = remote(mixed_ref, mixed_other, mix_send.at[0], mix_recv.at[0], partner)

    near_first = sorted(range(1, Z), key=lambda j: min(j, Z - j))
    for j in near_first:
        pass_on(j)

    loads["w"].wait()
    for one in weights:
        one.wait_recv()
    mixing.wait_recv()

    def part(target):
        columns = pl.ds(pl.multiple_of((2 * target + core) * WIDTH, WIDTH), WIDTH)
        return dot(mixed_ref[...], w_ref[:, columns], 1, 0) + dot(
            mixed_other[...], w_other[target], 1, 0
        )

    reduces = []
    for j in reversed(near_first):
        rs_send[j] = part(lax.rem(z + j, Z)).astype(BF16)
        reduces.append(
            remote(rs_send.at[j], rs_recv.at[j], r_send.at[j], r_recv.at[j], z_peer(j))
        )

    for one in passed:
        one.wait_recv()
    grad = jnp.zeros((LENGTH, WIDTH), F32)
    for i in range(2 * Z):
        grad = grad + dot(og_all[i], w_ref[:, i * WIDTH : (i + 1) * WIDTH], 1, 1)
    grad = jnp.where(live, grad.astype(BF16).astype(F32), 0.0)
    read_grad = gate * grad
    local_grad = ((1.0 - gate) * grad).astype(BF16)
    numer_grad = (read_grad * inverse).astype(BF16)
    product = read_grad * read_ref[...]
    denom_grad = -inverse * both(
        lambda h: jnp.broadcast_to(jnp.sum(product[:, h], axis=1, keepdims=True), (LENGTH, DH))
    )
    state_grad = both(lambda h: dot(sigq_ref[:, h], numer_grad[:, h], 0, 0))
    norm_grad = jnp.sum(phi(q_ref[...].astype(F32)) * denom_grad, axis=0, keepdims=True)
    backward.start(state_grad, norm_grad, flag)
    backward.send_first()

    parts = []
    for n in range(2):
        h = slice(n * DH, (n + 1) * DH)
        probs = probs_ref[n]
        probs_grad = dot(local_grad[:, h], v_ref[:, h], 1, 1)
        inner = jnp.sum(probs_grad * probs, axis=1, keepdims=True)
        scores_grad = (probs * (probs_grad - inner) * SCALE).astype(BF16)
        parts.append(
            (
                dot(scores_grad, k_ref[:, h], 1, 0)
                + (dot(numer_grad[:, h], f_in[:, h], 1, 1) + denom_grad[:, h] * norm_in[:, h])
                * phi_slope(q_ref[:, h].astype(F32)),
                dot(scores_grad, q_ref[:, h], 0, 0),
                dot(probs.astype(BF16), local_grad[:, h], 0, 0),
            )
        )
    stores = []

    def store(n, value, target):
        results[n] = value.astype(BF16)
        one = pltpu.make_async_copy(results.at[n], target, store_sem.at[n])
        one.start()
        stores.append(one)

    store(1, jnp.concatenate([parts[0][0], parts[1][0]], axis=1), dq_hbm)
    key_part = jnp.concatenate([parts[0][1], parts[1][1]], axis=1)
    value_part = jnp.concatenate([parts[0][2], parts[1][2]], axis=1)
    own = part(z)

    backward.second()
    norm_back = backward.third()
    mem_back = backward.finish()
    k_float = k_ref[...].astype(F32)
    key_more = (both(lambda h: dot(v_ref[:, h], mem_back[:, h], 1, 1)) + norm_back) * phi_slope(
        k_float
    )
    store(2, key_part + jnp.where(live, key_more, 0.0), dk_hbm)
    sigk_low = jnp.where(live, phi(k_float), 0.0).astype(BF16)
    store(3, value_part + both(lambda h: dot(sigk_low[:, h], mem_back[:, h], 1, 0)), dv_hbm)

    total = own
    for j, one in zip(reversed(near_first), reduces):
        one.wait_recv()
        total = total + rs_recv[j].astype(F32)
    store(0, total, out_hbm)

    for one in sent + forward.sent + backward.sent:
        one.wait_send()
    for one in stores:
        one.wait()


def store_all(*refs):
    sources, targets, held, sem = refs[:4], refs[4:8], refs[8], refs[9]
    loads = [pltpu.make_async_copy(sources[n], held.at[n], sem.at[0, n]) for n in range(4)]
    stores = [pltpu.make_async_copy(held.at[n], targets[n], sem.at[1, n]) for n in range(4)]
    for one in loads:
        one.start()
    for load, one in zip(loads, stores):
        load.wait()
        one.start()
    for one in stores:
        one.wait()


def build(mesh, X):
    Y, Z = mesh.shape["seq"] // X, mesh.shape["head"] // 2
    rows = LENGTH // X
    dma = pltpu.SemaphoreType.DMA

    def scan_scratch():
        return [
            pltpu.VMEM((X, rows + SMALL, WIDTH), BF16),
            pltpu.VMEM((X, rows + SMALL, WIDTH), BF16),
            pltpu.VMEM((rows + SMALL, WIDTH), BF16),
            pltpu.VMEM((Y, rows + SMALL, WIDTH), BF16),
            pltpu.VMEM((X, rows, WIDTH), BF16),
            pltpu.VMEM((LENGTH, WIDTH), BF16),
        ]

    def block():
        return pltpu.VMEM((LENGTH, WIDTH), BF16)

    def wide():
        return pltpu.VMEM((LENGTH, WIDTH), F32)

    most = max(X, Y)
    scratch = [
        pltpu.SMEM((2,), F32),
        pltpu.SMEM((1,), jnp.int32),
        pltpu.SMEM((1,), jnp.int32),
        block(),
        block(),
        block(),
        pltpu.VMEM((2 * Z, LENGTH, WIDTH), BF16),
        pltpu.VMEM((WIDTH, 2 * Z * WIDTH), BF16),
        pltpu.VMEM((Z, WIDTH, WIDTH), BF16),
        pltpu.VMEM((4, LENGTH, WIDTH), BF16),
        pltpu.VMEM((2, LENGTH, LENGTH), F32),
        wide(),
        block(),
        wide(),
        block(),
        block(),
        pltpu.VMEM((Z, LENGTH, WIDTH), BF16),
        pltpu.VMEM((Z, LENGTH, WIDTH), BF16),
        *scan_scratch(),
        *scan_scratch(),
        dma((8,)),
        dma((4,)),
        dma((3, most)),
        dma((3, most)),
        dma((3, most)),
        dma((3, most)),
        dma((Z,)),
        dma((Z,)),
        dma((Z,)),
        dma((Z,)),
        dma((Z,)),
        dma((Z,)),
        dma((1,)),
        dma((1,)),
        dma((Z,)),
        dma((Z,)),
    ]

    def shards(queries, keys, values, gate, out_weight, out_grad, valid, starts):
        one = jax.ShapeDtypeStruct((LENGTH, WIDTH), BF16)
        results = pl.pallas_call(
            functools.partial(layer, (X, Y, Z)),
            out_shape=(one,) * 4,
            in_specs=[pl.BlockSpec(memory_space=pltpu.HBM)] * 8,
            out_specs=(pl.BlockSpec(memory_space=pl.ANY),) * 4,
            scratch_shapes=scratch,
            compiler_params=pltpu.CompilerParams(
                collective_id=0, has_side_effects=True, vmem_limit_bytes=63 * 1024 * 1024
            ),
            name="layer",
        )(gate, valid, starts, queries, keys, values, out_grad, out_weight)
        return pl.pallas_call(
            store_all,
            out_shape=(one,) * 4,
            in_specs=[pl.BlockSpec(memory_space=pl.ANY)] * 4,
            out_specs=(pl.BlockSpec(memory_space=pltpu.HBM),) * 4,
            scratch_shapes=[pltpu.VMEM((4, LENGTH, WIDTH), BF16), dma((2, 4))],
            compiler_params=pltpu.CompilerParams(vmem_limit_bytes=63 * 1024 * 1024),
            name="store_all",
        )(*results)

    placed = (
        P("seq", "head"),
        P("seq", "head"),
        P("seq", "head"),
        P("head"),
        P("head", None),
        P("seq", "head"),
        P("seq"),
        P("seq"),
    )
    return jax.shard_map(
        shards, mesh=mesh, in_specs=placed, out_specs=(P("seq", "head"),) * 4, check_vma=False
    )


def solution(mesh):
    return build(mesh, 8)
```

```python
import functools

import jax
import jax.numpy as jnp
from jax import lax
from jax.experimental import pallas as pl
from jax.experimental.pallas import tpu as pltpu
from jax.sharding import PartitionSpec as P

DH = 128
LENGTH = 128
WIDTH = 2 * DH
SMALL = 16
SCALE = DH ** (-0.5)
MESH = pl.DeviceIdType.MESH
F32, BF16 = jnp.float32, jnp.bfloat16


def dot(a, b, contract_a, contract_b):
    return lax.dot_general(
        a, b, (((contract_a,), (contract_b,)), ((), ())), preferred_element_type=F32
    )


def phi(x):
    return jnp.where(x > 0, x + 1.0, jnp.exp(jnp.minimum(x, 0.0)))


def phi_slope(x):
    return jnp.where(x > 0, 1.0, jnp.where(x == 0, 0.5, jnp.exp(jnp.minimum(x, 0.0))))


def both(one):
    return jnp.concatenate([one(slice(0, DH)), one(slice(DH, WIDTH))], axis=1)


def small_rows(norm, flag):
    high = norm.astype(BF16).astype(F32)
    low = norm - high
    at = lax.broadcasted_iota(jnp.int32, (SMALL, DH), 0)
    rows = jnp.zeros((SMALL, DH), F32)
    for n, row in enumerate(
        (high[:, :DH], high[:, DH:], low[:, :DH], low[:, DH:], flag[:, :DH])
    ):
        rows = jnp.where(at == n, row, rows)
    return rows.astype(BF16)


def split_small(small):
    small = small.astype(F32)
    norm = jnp.concatenate([small[0:1] + small[2:3], small[1:2] + small[3:4]], axis=1)
    return norm, jnp.concatenate([small[4:5], small[4:5]], axis=1)


def layer(
    sizes,
    gate_hbm,
    valid_hbm,
    starts_hbm,
    q_hbm,
    k_hbm,
    v_hbm,
    og_hbm,
    w_hbm,
    out_hbm,
    dq_hbm,
    dk_hbm,
    dv_hbm,
    gate_ref,
    valid_ref,
    starts_ref,
    q_ref,
    k_ref,
    v_ref,
    og_all,
    w_ref,
    w_other,
    results,
    probs_ref,
    local_ref,
    sigq_ref,
    read_ref,
    mixed_ref,
    mixed_other,
    grad_theirs,
    grad_other,
    part_ref,
    rs_send,
    rs_recv,
    f_msg1,
    f_buf1,
    f_msg2,
    f_buf2,
    f_msg3,
    f_in,
    b_msg1,
    b_buf1,
    b_msg2,
    b_buf2,
    b_msg3,
    b_in,
    n_msg1,
    n_buf1,
    n_msg2,
    n_buf2,
    load_sem,
    store_sem,
    scan_send,
    scan_recv,
    ag_send,
    ag_recv,
    w_send,
    w_recv,
    swap_send,
    swap_recv,
    rs_send_sem,
    rs_recv_sem,
):
    X, Y, Z = sizes
    rows = LENGTH // X
    half = LENGTH // 2
    seq, head = lax.axis_index("seq"), lax.axis_index("head")
    y, x = lax.div(seq, X), lax.rem(seq, X)
    z, core = lax.div(head, 2), lax.rem(head, 2)

    def x_peer(j):
        return (y * X + lax.rem(x + j, X), head)

    def y_peer(j):
        return (lax.rem(y + j, Y) * X + x, head)

    def z_at(j):
        return lax.rem(z + j + Z, Z)

    def z_peer(j):
        return (seq, z_at(j) * 2 + core)

    partner = (seq, z * 2 + (1 - core))
    sent = []

    def remote(src, dst, send, recv, peer):
        one = pltpu.make_async_remote_copy(
            src_ref=src,
            dst_ref=dst,
            send_sem=send,
            recv_sem=recv,
            device_id=peer,
            device_id_type=MESH,
        )
        one.start()
        sent.append(one)
        return one

    loads = {}
    for n, (name, src, dst) in enumerate(
        (
            ("og", og_hbm, og_all.at[z]),
            ("k", k_hbm, k_ref),
            ("v", v_hbm, v_ref),
            ("valid", valid_hbm, valid_ref),
            ("starts", starts_hbm, starts_ref),
            ("gate", gate_hbm, gate_ref),
            ("q", q_hbm, q_ref),
            ("w", w_hbm, w_ref),
        )
    ):
        loads[name] = pltpu.make_async_copy(src, dst, load_sem.at[n])
        loads[name].start()

    barrier = pltpu.get_barrier_semaphore()
    peers = [x_peer(j) for j in range(1, X)] + [y_peer(j) for j in range(1, Y)]
    relayed = Z == 8
    straight = (2, 6, 1, 7) if relayed else tuple(range(1, Z))
    peers += [z_peer(j) for j in straight] + [partner]
    for peer in peers:
        pl.semaphore_signal(barrier, inc=1, device_id=peer, device_id_type=MESH)

    def along_x(phase, source, target):
        return [
            remote(
                source(lax.rem(x + j, X)),
                target,
                scan_send.at[phase, j],
                scan_recv.at[phase, j],
                x_peer(j),
            )
            for j in range(1, X)
        ]

    def along_y(phase, source, target):
        return [
            remote(source, target, scan_send.at[phase, j], scan_recv.at[phase, j], y_peer(j))
            for j in range(1, Y)
        ]

    def arrived(copies):
        for one in copies:
            one.wait_recv()

    def pack(ref, place, block):
        ref[place, 0:rows, :] = block[:, :DH]
        ref[place, rows : 2 * rows, :] = block[:, DH:]

    def unpack(ref, place):
        return jnp.concatenate(
            [ref[place, 0:rows, :], ref[place, rows : 2 * rows, :]], axis=1
        ).astype(F32)

    def small_of(ref, place):
        return split_small(ref[place, 2 * rows : 2 * rows + SMALL, :])

    zero_block, zero_row = jnp.zeros((rows, WIDTH), F32), jnp.zeros((1, WIDTH), F32)
    x_row, y_row = jnp.full((1, WIDTH), x, jnp.int32), jnp.full((1, WIDTH), y, jnp.int32)
    here = pl.ds(pl.multiple_of(x * rows, rows), rows)

    upper, lower, full = slice(0, half), slice(half, LENGTH), slice(0, LENGTH)

    def gather(n, block, part, to):
        piece = og_all.at[z_at(block), part]
        return remote(piece, piece, ag_send.at[n], ag_recv.at[n], z_peer(to))

    pl.semaphore_wait(barrier, len(peers))
    loads["og"].wait()
    gathers = {n: gather(n, 0, full, to) for n, to in enumerate(straight)}

    for name in ("valid", "starts", "gate"):
        loads[name].wait()
    live = lax.broadcasted_iota(jnp.int32, (LENGTH, WIDTH), 0) < valid_ref[0]
    flag = jnp.full((1, WIDTH), starts_ref[0], jnp.int32).astype(F32)
    lanes = lax.broadcasted_iota(jnp.int32, (1, WIDTH), 1)
    logit = jnp.where(
        lanes < DH, jnp.full((1, WIDTH), gate_ref[0], F32), jnp.full((1, WIDTH), gate_ref[1], F32)
    )
    gate = 1.0 / (1.0 + jnp.exp(-logit))

    loads["k"].wait()
    sigk = jnp.where(live, phi(k_ref[...].astype(F32)), 0.0)
    sigk_low = sigk.astype(BF16)
    loads["v"].wait()
    state = both(lambda h: dot(sigk_low[:, h], v_ref[:, h], 0, 0)).astype(BF16)
    small = small_rows(jnp.sum(sigk, axis=0, keepdims=True), flag)
    for i in range(X):
        pack(f_msg1, i, state[i * rows : (i + 1) * rows])
        f_msg1[i, 2 * rows :, :] = small
    f_buf1[x] = f_msg1[x]

    first = along_x(0, lambda to: f_msg1.at[to], f_buf1.at[x])

    weights = []
    for i in range(Z):
        columns = pl.ds(pl.multiple_of((2 * i + 1 - core) * WIDTH, WIDTH), WIDTH)
        weights.append(
            remote(w_hbm.at[:, columns], w_other.at[i], w_send.at[i], w_recv.at[i], partner)
        )

    loads["q"].wait()
    row = lax.broadcasted_iota(jnp.int32, (LENGTH, LENGTH), 0)
    col = lax.broadcasted_iota(jnp.int32, (LENGTH, LENGTH), 1)
    allowed = (col <= row) & (col < valid_ref[0])
    for n in range(2):
        h = slice(n * DH, (n + 1) * DH)
        scores = dot(q_ref[:, h], k_ref[:, h], 1, 1) * SCALE
        scores = jnp.where(allowed, scores, -1e30)
        expo = jnp.exp(scores - jnp.max(scores, axis=1, keepdims=True))
        probs = expo / jnp.sum(expo, axis=1, keepdims=True)
        probs_ref[n] = probs
        local_ref[:, h] = dot(probs.astype(BF16), v_ref[:, h], 1, 0)

    if relayed:
        for n, (came, block, part, to) in enumerate(
            ((0, -2, upper, 2), (0, -2, full, 1), (1, 2, lower, -2), (1, 2, full, -1))
        ):
            if n % 2 == 0:
                gathers[came].wait_recv()
            gathers[4 + n] = gather(4 + n, block, part, to)

    arrived(first)
    acc, acc_norm, still_open = zero_block, zero_row, jnp.ones((1, WIDTH), F32)
    for i in range(X):
        norm, start = small_of(f_buf1, i)
        opened = 1.0 - start
        acc = opened * acc + unpack(f_buf1, i)
        acc_norm = opened * acc_norm + norm
        still_open = still_open * opened
    pack(f_msg2, 0, acc.astype(BF16))
    f_msg2[0, 2 * rows :, :] = small_rows(acc_norm, still_open)
    f_buf2[y] = f_msg2[0]
    second = along_y(1, f_msg2.at[0], f_buf2.at[y])

    sigq = phi(q_ref[...].astype(F32))
    sigq_ref[...] = sigq.astype(BF16)

    def cotangent(j):
        block = z_at(j)
        columns = pl.ds(pl.multiple_of((2 * block + core) * WIDTH, WIDTH), WIDTH)
        return (
            dot(og_all[block], w_ref[:, columns], 1, 1),
            dot(og_all[block], w_other[block], 1, 1),
        )

    loads["w"].wait()
    arrived(weights)
    mine, theirs = cotangent(0)
    steps = ((0, 2), (1, 6), (2, 1), (3, 7)) if relayed else enumerate(straight)
    for n, to in steps:
        if not relayed or n > 1:
            gathers[n].wait_recv()
        more, more_theirs = cotangent(-to)
        mine, theirs = mine + more, theirs + more_theirs
    if relayed:
        for came, block in (((5,), -3), ((7,), 3), ((4, 6), 4)):
            for n in came:
                gathers[n].wait_recv()
            more, more_theirs = cotangent(block)
            mine, theirs = mine + more, theirs + more_theirs
    grad_theirs[...] = theirs
    swap = remote(grad_theirs, grad_other, swap_send.at[0], swap_recv.at[0], partner)

    arrived(second)
    acc, acc_norm = zero_block, zero_row
    for i in range(Y):
        norm, still_open = small_of(f_buf2, i)
        counts = y_row > i
        acc = jnp.where(counts, unpack(f_buf2, i) + still_open * acc, acc)
        acc_norm = jnp.where(counts, norm + still_open * acc_norm, acc_norm)
    norm_in = zero_row
    for i in range(X):
        norm, start = small_of(f_buf1, i)
        opened = 1.0 - start
        acc, acc_norm = opened * acc, opened * acc_norm
        f_msg3[i] = acc.astype(BF16)
        norm_in = jnp.where(x_row == i, acc_norm, norm_in)
        acc, acc_norm = acc + unpack(f_buf1, i), acc_norm + norm
    f_in[here, :] = f_msg3[x]
    third = along_x(2, lambda to: f_msg3.at[to], f_in.at[here, :])

    scaled = sigq * norm_in
    inverse = both(
        lambda h: jnp.broadcast_to(
            1.0 / (jnp.sum(scaled[:, h], axis=1, keepdims=True) + 1.0), (LENGTH, DH)
        )
    )

    swap.wait_recv()
    grad = jnp.where(live, (mine + grad_other[...]).astype(BF16).astype(F32), 0.0)
    read_grad = gate * grad
    local_grad = ((1.0 - gate) * grad).astype(BF16)
    numer_grad = (read_grad * inverse).astype(BF16)
    state_grad = both(lambda h: dot(sigq_ref[:, h], numer_grad[:, h], 0, 0)).astype(BF16)
    for i in range(X):
        pack(b_msg1, i, state_grad[i * rows : (i + 1) * rows])
    b_buf1[x] = b_msg1[x]
    b_first = along_x(3, lambda to: b_msg1.at[to], b_buf1.at[x])

    arrived(third)
    read = both(lambda h: dot(sigq_ref[:, h], f_in[:, h], 1, 0)) * inverse
    mixed = jnp.where(live, gate * read + (1.0 - gate) * local_ref[...], 0.0)
    mixed_ref[...] = mixed.astype(BF16)
    mixing = remote(mixed_ref, mixed_other, swap_send.at[1], swap_recv.at[1], partner)

    product = read_grad * read
    denom_grad = -inverse * both(
        lambda h: jnp.broadcast_to(jnp.sum(product[:, h], axis=1, keepdims=True), (LENGTH, DH))
    )
    n_msg1[...] = small_rows(jnp.sum(sigq * denom_grad, axis=0, keepdims=True), flag)
    n_buf1[x] = n_msg1[...]
    n_first = along_x(6, lambda to: n_msg1, n_buf1.at[x])

    for j in range(Z):
        columns = pl.ds(pl.multiple_of((2 * z_at(j) + core) * WIDTH, WIDTH), WIDTH)
        part_ref[j] = dot(mixed_ref[...], w_ref[:, columns], 1, 0)

    arrived(b_first)
    acc = zero_block
    for i in range(X - 1, -1, -1):
        _, start = small_of(f_buf1, i)
        acc = (1.0 - start) * (acc + unpack(b_buf1, i))
    pack(b_msg2, 0, acc.astype(BF16))
    b_buf2[y] = b_msg2[0]
    b_second = along_y(4, b_msg2.at[0], b_buf2.at[y])

    mixing.wait_recv()
    reduces = {}

    def whole(j):
        j = j % Z
        return part_ref[j] + dot(mixed_other[...], w_other[z_at(j)], 1, 0)

    def reduce(n, value, part, to):
        rs_send[n, part] = value.astype(BF16)
        reduces[n] = remote(
            rs_send.at[n, part],
            rs_recv.at[n, part],
            rs_send_sem.at[n],
            rs_recv_sem.at[n],
            z_peer(to),
        )

    if relayed:
        across = whole(4)
        reduce(4, across[upper], upper, 2)
        reduce(6, across[lower], lower, -2)
        reduce(5, whole(3), full, 1)
        reduce(7, whole(-3), full, -1)
        reduce(2, whole(1), full, 1)
        reduce(3, whole(-1), full, -1)
        part_ref[2] = whole(2)
        part_ref[6] = whole(6)
    else:
        for n, to in enumerate(straight):
            reduce(n, whole(to), full, to)
    part_ref[0] = whole(0)

    parts = []
    for n in range(2):
        h = slice(n * DH, (n + 1) * DH)
        probs = probs_ref[n]
        probs_grad = dot(local_grad[:, h], v_ref[:, h], 1, 1)
        inner = jnp.sum(probs_grad * probs, axis=1, keepdims=True)
        scores_grad = (probs * (probs_grad - inner) * SCALE).astype(BF16)
        parts.append(
            (
                dot(scores_grad, k_ref[:, h], 1, 0)
                + (dot(numer_grad[:, h], f_in[:, h], 1, 1) + denom_grad[:, h] * norm_in[:, h])
                * phi_slope(q_ref[:, h].astype(F32)),
                dot(scores_grad, q_ref[:, h], 0, 0),
                dot(probs.astype(BF16), local_grad[:, h], 0, 0),
            )
        )
    stores = []

    def store(n, value, target):
        results[n] = value.astype(BF16)
        one = pltpu.make_async_copy(results.at[n], target, store_sem.at[n])
        one.start()
        stores.append(one)

    store(1, jnp.concatenate([parts[0][0], parts[1][0]], axis=1), dq_hbm)
    key_part = jnp.concatenate([parts[0][1], parts[1][1]], axis=1)
    value_part = jnp.concatenate([parts[0][2], parts[1][2]], axis=1)

    arrived(n_first)
    acc_norm = zero_row
    for i in range(X - 1, -1, -1):
        _, start = small_of(f_buf1, i)
        acc_norm = (1.0 - start) * (acc_norm + split_small(n_buf1[i])[0])
    n_msg2[...] = small_rows(acc_norm, flag)
    n_buf2[y] = n_msg2[...]
    n_second = along_y(7, n_msg2, n_buf2.at[y])

    arrived(b_second)
    acc = zero_block
    for i in range(Y - 1, -1, -1):
        _, still_open = small_of(f_buf2, i)
        acc = jnp.where(y_row < i, unpack(b_buf2, i) + still_open * acc, acc)
    for i in range(X - 1, -1, -1):
        _, start = small_of(f_buf1, i)
        b_msg3[i] = acc.astype(BF16)
        acc = (1.0 - start) * (acc + unpack(b_buf1, i))
    b_in[here, :] = b_msg3[x]
    b_third = along_x(5, lambda to: b_msg3.at[to], b_in.at[here, :])

    if relayed:
        for n, straight_on, across, part, to in ((0, 5, 4, upper, 2), (1, 7, 6, lower, -2)):
            reduces[straight_on].wait_recv()
            reduces[across].wait_recv()
            j = to % Z
            part_ref[j] = part_ref[j] + rs_recv[straight_on].astype(F32)
            part_ref[j, part] = part_ref[j, part] + rs_recv[across, part].astype(F32)
            reduce(n, part_ref[j], full, to)

    arrived(n_second)
    acc_norm = zero_row
    for i in range(Y - 1, -1, -1):
        _, still_open = small_of(f_buf2, i)
        acc_norm = jnp.where(
            y_row < i, split_small(n_buf2[i])[0] + still_open * acc_norm, acc_norm
        )
    norm_back = zero_row
    for i in range(X - 1, -1, -1):
        _, start = small_of(f_buf1, i)
        norm_back = jnp.where(x_row == i, acc_norm, norm_back)
        acc_norm = (1.0 - start) * (acc_norm + split_small(n_buf1[i])[0])

    arrived(b_third)
    k_float = k_ref[...].astype(F32)
    key_more = (both(lambda h: dot(v_ref[:, h], b_in[:, h], 1, 1)) + norm_back) * phi_slope(k_float)
    store(2, key_part + jnp.where(live, key_more, 0.0), dk_hbm)
    sigk_low = jnp.where(live, phi(k_float), 0.0).astype(BF16)
    store(3, value_part + both(lambda h: dot(sigk_low[:, h], b_in[:, h], 1, 0)), dv_hbm)

    total = part_ref[0]
    for n in (2, 3, 0, 1) if relayed else range(Z - 1):
        reduces[n].wait_recv()
        total = total + rs_recv[n].astype(F32)
    store(0, total, out_hbm)

    for one in sent:
        one.wait_send()
    for one in stores:
        one.wait()


def store_all(*refs):
    sources, targets, held, sem = refs[:4], refs[4:8], refs[8], refs[9]
    loads = [pltpu.make_async_copy(sources[n], held.at[n], sem.at[0, n]) for n in range(4)]
    stores = [pltpu.make_async_copy(held.at[n], targets[n], sem.at[1, n]) for n in range(4)]
    for one in loads:
        one.start()
    for load, one in zip(loads, stores):
        load.wait()
        one.start()
    for one in stores:
        one.wait()


def build(mesh, X):
    Y, Z = mesh.shape["seq"] // X, mesh.shape["head"] // 2
    rows = LENGTH // X
    dma = pltpu.SemaphoreType.DMA

    def block(*lead):
        return pltpu.VMEM((*lead, LENGTH, WIDTH), BF16)

    def wide(*lead):
        return pltpu.VMEM((*lead, LENGTH, WIDTH), F32)

    def message(n, count):
        return pltpu.VMEM((n, count, DH), BF16)

    most = max(X, Y)
    full = 2 * rows + SMALL
    scratch = [
        pltpu.SMEM((2,), F32),
        pltpu.SMEM((1,), jnp.int32),
        pltpu.SMEM((1,), jnp.int32),
        block(),
        block(),
        block(),
        block(Z),
        pltpu.VMEM((WIDTH, 2 * Z * WIDTH), BF16),
        pltpu.VMEM((Z, WIDTH, WIDTH), BF16),
        block(4),
        pltpu.VMEM((2, LENGTH, LENGTH), F32),
        wide(),
        block(),
        wide(),
        block(),
        block(),
        wide(),
        wide(),
        wide(Z),
        block(8),
        block(8),
        message(X, full),
        message(X, full),
        message(1, full),
        message(Y, full),
        pltpu.VMEM((X, rows, WIDTH), BF16),
        block(),
        message(X, 2 * rows),
        message(X, 2 * rows),
        message(1, 2 * rows),
        message(Y, 2 * rows),
        pltpu.VMEM((X, rows, WIDTH), BF16),
        block(),
        pltpu.VMEM((SMALL, DH), BF16),
        message(X, SMALL),
        pltpu.VMEM((SMALL, DH), BF16),
        message(Y, SMALL),
        dma((8,)),
        dma((4,)),
        dma((8, most)),
        dma((8, most)),
        dma((8,)),
        dma((8,)),
        dma((Z,)),
        dma((Z,)),
        dma((2,)),
        dma((2,)),
        dma((8,)),
        dma((8,)),
    ]

    def shards(queries, keys, values, gate, out_weight, out_grad, valid, starts):
        one = jax.ShapeDtypeStruct((LENGTH, WIDTH), BF16)
        results = pl.pallas_call(
            functools.partial(layer, (X, Y, Z)),
            out_shape=(one,) * 4,
            in_specs=[pl.BlockSpec(memory_space=pltpu.HBM)] * 8,
            out_specs=(pl.BlockSpec(memory_space=pl.ANY),) * 4,
            scratch_shapes=scratch,
            compiler_params=pltpu.CompilerParams(
                collective_id=0, has_side_effects=True, vmem_limit_bytes=63 * 1024 * 1024
            ),
            name="layer",
        )(gate, valid, starts, queries, keys, values, out_grad, out_weight)
        return pl.pallas_call(
            store_all,
            out_shape=(one,) * 4,
            in_specs=[pl.BlockSpec(memory_space=pl.ANY)] * 4,
            out_specs=(pl.BlockSpec(memory_space=pltpu.HBM),) * 4,
            scratch_shapes=[pltpu.VMEM((4, LENGTH, WIDTH), BF16), dma((2, 4))],
            compiler_params=pltpu.CompilerParams(vmem_limit_bytes=63 * 1024 * 1024),
            name="store_all",
        )(*results)

    placed = (
        P("seq", "head"),
        P("seq", "head"),
        P("seq", "head"),
        P("head"),
        P("head", None),
        P("seq", "head"),
        P("seq"),
        P("seq"),
    )
    return jax.shard_map(
        shards, mesh=mesh, in_specs=placed, out_specs=(P("seq", "head"),) * 4, check_vma=False
    )


def solution(mesh):
    return build(mesh, 8)
```

```python
import functools

import jax
import jax.numpy as jnp
from jax import lax
from jax.experimental import pallas as pl
from jax.experimental.pallas import tpu as pltpu
from jax.sharding import PartitionSpec as P

DH = 128
LENGTH = 128
WIDTH = 2 * DH
SMALL = 16
SCALE = DH ** (-0.5)
MESH = pl.DeviceIdType.MESH
F32, BF16 = jnp.float32, jnp.bfloat16


def dot(a, b, contract_a, contract_b):
    return lax.dot_general(
        a, b, (((contract_a,), (contract_b,)), ((), ())), preferred_element_type=F32
    )


def phi(x):
    return jnp.where(x > 0, x + 1.0, jnp.exp(jnp.minimum(x, 0.0)))


def phi_slope(x):
    return jnp.where(x > 0, 1.0, jnp.where(x == 0, 0.5, jnp.exp(jnp.minimum(x, 0.0))))


def both(one):
    return jnp.concatenate([one(slice(0, DH)), one(slice(DH, WIDTH))], axis=1)


def small_rows(norm, flag):
    high = norm.astype(BF16).astype(F32)
    low = norm - high
    at = lax.broadcasted_iota(jnp.int32, (SMALL, DH), 0)
    rows = jnp.zeros((SMALL, DH), F32)
    for n, row in enumerate(
        (high[:, :DH], high[:, DH:], low[:, :DH], low[:, DH:], flag[:, :DH])
    ):
        rows = jnp.where(at == n, row, rows)
    return rows.astype(BF16)


def split_small(small):
    small = small.astype(F32)
    norm = jnp.concatenate([small[0:1] + small[2:3], small[1:2] + small[3:4]], axis=1)
    return norm, jnp.concatenate([small[4:5], small[4:5]], axis=1)


def layer(
    sizes,
    valid_ref,
    starts_ref,
    gate_hbm,
    q_hbm,
    k_hbm,
    v_hbm,
    og_hbm,
    w_hbm,
    out_ref,
    dq_ref,
    dk_ref,
    dv_ref,
    gate_ref,
    q_ref,
    k_ref,
    v_ref,
    og_all,
    w_blocks,
    probs_ref,
    local_ref,
    sigq_ref,
    read_ref,
    mixed_ref,
    mixed_other,
    grad_theirs,
    grad_other,
    part_ref,
    rs_send,
    rs_recv,
    f_msg1,
    f_buf1,
    f_msg2,
    f_buf2,
    f_msg3,
    f_in,
    b_msg1,
    b_buf1,
    b_msg2,
    b_buf2,
    b_msg3,
    b_in,
    s_msg1,
    s_buf1,
    s_msg2,
    s_buf2,
    n_msg1,
    n_buf1,
    n_msg2,
    n_buf2,
    load_sem,
    own_sem,
    scan_send,
    scan_recv,
    ag_send,
    ag_recv,
    w_send,
    w_recv,
    swap_send,
    swap_recv,
    rs_send_sem,
    rs_recv_sem,
):
    X, Y, Z = sizes
    rows = LENGTH // X
    half = LENGTH // 2
    seq, head = lax.axis_index("seq"), lax.axis_index("head")
    y, x = lax.div(seq, X), lax.rem(seq, X)
    z, core = lax.div(head, 2), lax.rem(head, 2)

    def x_peer(j):
        return (y * X + lax.rem(x + j, X), head)

    def y_peer(j):
        return (lax.rem(y + j, Y) * X + x, head)

    def z_at(j):
        return lax.rem(z + j + Z, Z)

    def z_peer(j):
        return (seq, z_at(j) * 2 + core)

    partner = (seq, z * 2 + (1 - core))
    sent = []

    def remote(src, dst, send, recv, peer):
        one = pltpu.make_async_remote_copy(
            src_ref=src,
            dst_ref=dst,
            send_sem=send,
            recv_sem=recv,
            device_id=peer,
            device_id_type=MESH,
        )
        one.start()
        sent.append(one)
        return one

    loads = {}
    for n, (name, src, dst) in enumerate(
        (
            ("og", og_hbm, og_all.at[z]),
            ("k", k_hbm, k_ref),
            ("v", v_hbm, v_ref),
            ("gate", gate_hbm, gate_ref),
            ("q", q_hbm, q_ref),
        )
    ):
        loads[name] = pltpu.make_async_copy(src, dst, load_sem.at[n])
        loads[name].start()

    barrier = pltpu.get_barrier_semaphore()
    peers = [x_peer(j) for j in range(1, X)] + [y_peer(j) for j in range(1, Y)]
    relayed = Z == 8
    straight = (2, 6, 1, 7) if relayed else tuple(range(1, Z))
    peers += [z_peer(j) for j in straight] + [partner]
    for peer in peers:
        pl.semaphore_signal(barrier, inc=1, device_id=peer, device_id_type=MESH)

    def far_first(n):
        return sorted(range(1, n), key=lambda j: -min(j, n - j))

    def along_x(phase, source, target):
        return [
            remote(
                source(lax.rem(x + j, X)),
                target,
                scan_send.at[phase, j],
                scan_recv.at[phase, j],
                x_peer(j),
            )
            for j in far_first(X)
        ]

    def along_y(phase, source, target):
        return [
            remote(source, target, scan_send.at[phase, j], scan_recv.at[phase, j], y_peer(j))
            for j in far_first(Y)
        ]

    def arrived(copies):
        for one in copies:
            one.wait_recv()

    def pack(ref, place, block):
        ref[place, 0:rows, :] = block[:, :DH]
        ref[place, rows : 2 * rows, :] = block[:, DH:]

    def unpack(ref, place):
        return jnp.concatenate(
            [ref[place, 0:rows, :], ref[place, rows : 2 * rows, :]], axis=1
        ).astype(F32)

    zero_block, zero_row = jnp.zeros((rows, WIDTH), F32), jnp.zeros((1, WIDTH), F32)
    x_row, y_row = jnp.full((1, WIDTH), x, jnp.int32), jnp.full((1, WIDTH), y, jnp.int32)
    here = pl.ds(pl.multiple_of(x * rows, rows), rows)

    upper, lower, full = slice(0, half), slice(half, LENGTH), slice(0, LENGTH)

    def gather(n, block, part, to):
        piece = og_all.at[z_at(block), part]
        return remote(piece, piece, ag_send.at[n], ag_recv.at[n], z_peer(to))

    pl.semaphore_wait(barrier, len(peers))
    loads["og"].wait()
    gathers = {n: gather(n, 0, full, to) for n, to in enumerate(straight)}

    live = lax.broadcasted_iota(jnp.int32, (LENGTH, WIDTH), 0) < valid_ref[0]
    flag = jnp.full((1, WIDTH), starts_ref[0], jnp.int32).astype(F32)
    loads["k"].wait()
    sigk = jnp.where(live, phi(k_ref[...].astype(F32)), 0.0)
    s_msg1[...] = small_rows(jnp.sum(sigk, axis=0, keepdims=True), flag)
    s_buf1[x] = s_msg1[...]
    s_first = along_x(8, lambda to: s_msg1, s_buf1.at[x])
    sigk_low = sigk.astype(BF16)
    loads["v"].wait()
    state = both(lambda h: dot(sigk_low[:, h], v_ref[:, h], 0, 0)).astype(BF16)
    for i in range(X):
        pack(f_msg1, i, state[i * rows : (i + 1) * rows])
    f_buf1[x] = f_msg1[x]
    first = along_x(0, lambda to: f_msg1.at[to], f_buf1.at[x])

    weights, own_weights = [], []
    for i in range(Z):
        columns = pl.ds(pl.multiple_of((2 * i + 1 - core) * WIDTH, WIDTH), WIDTH)
        weights.append(
            remote(
                w_hbm.at[:, columns],
                w_blocks.at[i, WIDTH:, :],
                w_send.at[i],
                w_recv.at[i],
                partner,
            )
        )
    for i in range(Z):
        columns = pl.ds(pl.multiple_of((2 * i + core) * WIDTH, WIDTH), WIDTH)
        own_weights.append(
            pltpu.make_async_copy(w_hbm.at[:, columns], w_blocks.at[i, 0:WIDTH, :], own_sem.at[i])
        )
        own_weights[i].start()

    loads["gate"].wait()
    lanes = lax.broadcasted_iota(jnp.int32, (1, WIDTH), 1)
    logit = jnp.where(
        lanes < DH, jnp.full((1, WIDTH), gate_ref[0], F32), jnp.full((1, WIDTH), gate_ref[1], F32)
    )
    gate = 1.0 / (1.0 + jnp.exp(-logit))

    loads["q"].wait()
    row = lax.broadcasted_iota(jnp.int32, (LENGTH, LENGTH), 0)
    col = lax.broadcasted_iota(jnp.int32, (LENGTH, LENGTH), 1)
    allowed = (col <= row) & (col < valid_ref[0])

    def attend(n):
        h = slice(n * DH, (n + 1) * DH)
        scores = dot(q_ref[:, h], k_ref[:, h], 1, 1) * SCALE
        scores = jnp.where(allowed, scores, -1e30)
        expo = jnp.exp(scores - jnp.max(scores, axis=1, keepdims=True))
        probs = expo / jnp.sum(expo, axis=1, keepdims=True)
        probs_ref[n] = probs
        local_ref[:, h] = dot(probs.astype(BF16), v_ref[:, h], 1, 0)

    attend(0)
    if relayed:
        for n, (came, block, part, to) in enumerate(
            ((0, -2, upper, 2), (0, -2, full, 1), (1, 2, lower, -2), (1, 2, full, -1))
        ):
            if n % 2 == 0:
                gathers[came].wait_recv()
            gathers[4 + n] = gather(4 + n, block, part, to)

    arrived(s_first)
    row_small = [split_small(s_buf1[i]) for i in range(X)]
    opened = [1.0 - start for _, start in row_small]
    acc_norm, still_open = zero_row, jnp.ones((1, WIDTH), F32)
    for i in range(X):
        acc_norm = opened[i] * acc_norm + row_small[i][0]
        still_open = still_open * opened[i]
    s_msg2[...] = small_rows(acc_norm, still_open)
    s_buf2[y] = s_msg2[...]
    s_second = along_y(9, s_msg2, s_buf2.at[y])

    attend(1)

    arrived(first)
    acc = zero_block
    for i in range(X):
        acc = opened[i] * acc + unpack(f_buf1, i)
    pack(f_msg2, 0, acc.astype(BF16))
    f_buf2[y] = f_msg2[0]
    second = along_y(1, f_msg2.at[0], f_buf2.at[y])

    sigq = phi(q_ref[...].astype(F32))
    sigq_ref[...] = sigq.astype(BF16)

    def cotangent(j):
        block = z_at(j)
        return dot(w_blocks[block], og_all[block], 1, 1)

    for one in own_weights:
        one.wait()
    arrived(weights)
    grads = cotangent(0)
    steps = ((0, 2), (1, 6), (2, 1), (3, 7)) if relayed else enumerate(straight)
    for n, to in steps:
        if not relayed or n > 1:
            gathers[n].wait_recv()
        grads = grads + cotangent(-to)
    if relayed:
        for came, block in (((5,), -3), ((7,), 3), ((4, 6), 4)):
            for n in came:
                gathers[n].wait_recv()
            grads = grads + cotangent(block)
    mine = grads[:WIDTH]
    grad_theirs[...] = grads[WIDTH:]
    swap = remote(grad_theirs, grad_other, swap_send.at[0], swap_recv.at[0], partner)

    arrived(s_second)
    rows_small = [split_small(s_buf2[i]) for i in range(Y)]
    acc_norm, norm_in = zero_row, zero_row
    for i in range(Y):
        norm, still_open = rows_small[i]
        acc_norm = jnp.where(y_row > i, norm + still_open * acc_norm, acc_norm)
    for i in range(X):
        acc_norm = opened[i] * acc_norm
        norm_in = jnp.where(x_row == i, acc_norm, norm_in)
        acc_norm = acc_norm + row_small[i][0]
    scaled = sigq * norm_in
    inverse = both(
        lambda h: jnp.broadcast_to(
            1.0 / (jnp.sum(scaled[:, h], axis=1, keepdims=True) + 1.0), (LENGTH, DH)
        )
    )

    arrived(second)
    acc = zero_block
    for i in range(Y):
        acc = jnp.where(y_row > i, unpack(f_buf2, i) + rows_small[i][1] * acc, acc)
    for i in range(X):
        acc = opened[i] * acc
        f_msg3[i] = acc.astype(BF16)
        acc = acc + unpack(f_buf1, i)
    f_in[here, :] = f_msg3[x]
    third = along_x(2, lambda to: f_msg3.at[to], f_in.at[here, :])

    gated = jnp.where(live, gate * inverse, 0.0)
    mixed_local = jnp.where(live, (1.0 - gate) * local_ref[...], 0.0)

    swap.wait_recv()
    grad = jnp.where(live, (mine + grad_other[...]).T.astype(BF16).astype(F32), 0.0)
    read_grad = gate * grad
    local_grad = ((1.0 - gate) * grad).astype(BF16)
    numer_grad = (gated * grad).astype(BF16)
    state_grad = both(lambda h: dot(sigq_ref[:, h], numer_grad[:, h], 0, 0)).astype(BF16)
    for i in range(X):
        pack(b_msg1, i, state_grad[i * rows : (i + 1) * rows])
    b_buf1[x] = b_msg1[x]
    b_first = along_x(3, lambda to: b_msg1.at[to], b_buf1.at[x])

    arrived(third)
    numer = both(lambda h: dot(sigq_ref[:, h], f_in[:, h], 1, 0))
    mixed_ref[...] = (gated * numer + mixed_local).astype(BF16)
    mixing = remote(mixed_ref, mixed_other, swap_send.at[1], swap_recv.at[1], partner)

    product = read_grad * (numer * inverse)
    denom_grad = -inverse * both(
        lambda h: jnp.broadcast_to(jnp.sum(product[:, h], axis=1, keepdims=True), (LENGTH, DH))
    )
    n_msg1[...] = small_rows(jnp.sum(sigq * denom_grad, axis=0, keepdims=True), flag)
    n_buf1[x] = n_msg1[...]
    n_first = along_x(6, lambda to: n_msg1, n_buf1.at[x])

    arrived(b_first)
    acc = zero_block
    for i in range(X - 1, -1, -1):
        acc = opened[i] * (acc + unpack(b_buf1, i))
    pack(b_msg2, 0, acc.astype(BF16))
    b_buf2[y] = b_msg2[0]
    b_second = along_y(4, b_msg2.at[0], b_buf2.at[y])

    reduce_order = [j for j in (4, 3, 5, 1, 7, 2, 6, 0) if relayed] or list(range(Z))
    for j in reduce_order[:3]:
        part_ref[j] = dot(mixed_ref[...], w_blocks[z_at(j), 0:WIDTH, :], 1, 0)

    mixing.wait_recv()
    reduces = {}

    def whole(j):
        j = j % Z
        block = z_at(j)
        if j in reduce_order[:3]:
            part = part_ref[j]
        else:
            part = dot(mixed_ref[...], w_blocks[block, 0:WIDTH, :], 1, 0)
        return part + dot(mixed_other[...], w_blocks[block, WIDTH:, :], 1, 0)

    def reduce(n, value, part, to):
        rs_send[n, part] = value.astype(BF16)
        reduces[n] = remote(
            rs_send.at[n, part],
            rs_recv.at[n, part],
            rs_send_sem.at[n],
            rs_recv_sem.at[n],
            z_peer(to),
        )

    if relayed:
        across = whole(4)
        reduce(4, across[upper], upper, 2)
        reduce(6, across[lower], lower, -2)
        reduce(5, whole(3), full, 1)
        reduce(7, whole(-3), full, -1)
        reduce(2, whole(1), full, 1)
        reduce(3, whole(-1), full, -1)
        part_ref[2] = whole(2)
        part_ref[6] = whole(6)
    else:
        for n, to in enumerate(straight):
            reduce(n, whole(to), full, to)
    part_ref[0] = whole(0)

    parts = []
    for n in range(2):
        h = slice(n * DH, (n + 1) * DH)
        probs = probs_ref[n]
        probs_grad = dot(local_grad[:, h], v_ref[:, h], 1, 1)
        inner = jnp.sum(probs_grad * probs, axis=1, keepdims=True)
        scores_grad = (probs * (probs_grad - inner) * SCALE).astype(BF16)
        parts.append(
            (
                dot(scores_grad, k_ref[:, h], 1, 0)
                + (dot(numer_grad[:, h], f_in[:, h], 1, 1) + denom_grad[:, h] * norm_in[:, h])
                * phi_slope(q_ref[:, h].astype(F32)),
                dot(scores_grad, q_ref[:, h], 0, 0),
                dot(probs.astype(BF16), local_grad[:, h], 0, 0),
            )
        )
    dq_ref[...] = jnp.concatenate([parts[0][0], parts[1][0]], axis=1).astype(BF16)
    key_part = jnp.concatenate([parts[0][1], parts[1][1]], axis=1)
    value_part = jnp.concatenate([parts[0][2], parts[1][2]], axis=1)

    arrived(n_first)
    acc_norm = zero_row
    for i in range(X - 1, -1, -1):
        acc_norm = opened[i] * (acc_norm + split_small(n_buf1[i])[0])
    n_msg2[...] = small_rows(acc_norm, flag)
    n_buf2[y] = n_msg2[...]
    n_second = along_y(7, n_msg2, n_buf2.at[y])

    arrived(b_second)
    acc = zero_block
    for i in range(Y - 1, -1, -1):
        acc = jnp.where(y_row < i, unpack(b_buf2, i) + rows_small[i][1] * acc, acc)
    for i in range(X - 1, -1, -1):
        b_msg3[i] = acc.astype(BF16)
        acc = opened[i] * (acc + unpack(b_buf1, i))
    b_in[here, :] = b_msg3[x]
    b_third = along_x(5, lambda to: b_msg3.at[to], b_in.at[here, :])

    if relayed:
        for n, straight_on, across, part, to in ((0, 5, 4, upper, 2), (1, 7, 6, lower, -2)):
            reduces[straight_on].wait_recv()
            reduces[across].wait_recv()
            j = to % Z
            part_ref[j] = part_ref[j] + rs_recv[straight_on].astype(F32)
            part_ref[j, part] = part_ref[j, part] + rs_recv[across, part].astype(F32)
            reduce(n, part_ref[j], full, to)

    arrived(n_second)
    acc_norm = zero_row
    for i in range(Y - 1, -1, -1):
        acc_norm = jnp.where(
            y_row < i, split_small(n_buf2[i])[0] + rows_small[i][1] * acc_norm, acc_norm
        )
    norm_back = zero_row
    for i in range(X - 1, -1, -1):
        norm_back = jnp.where(x_row == i, acc_norm, norm_back)
        acc_norm = opened[i] * (acc_norm + split_small(n_buf1[i])[0])

    k_float = k_ref[...].astype(F32)
    slope = jnp.where(live, phi_slope(k_float), 0.0)
    sigk_low = jnp.where(live, phi(k_float), 0.0).astype(BF16)
    key_part = key_part + norm_back * slope
    arrived(b_third)
    key_more = both(lambda h: dot(v_ref[:, h], b_in[:, h], 1, 1)) * slope
    dk_ref[...] = (key_part + key_more).astype(BF16)
    value_more = both(lambda h: dot(sigk_low[:, h], b_in[:, h], 1, 0))
    dv_ref[...] = (value_part + value_more).astype(BF16)

    total = part_ref[0]
    for n in (2, 3, 0, 1) if relayed else range(Z - 1):
        reduces[n].wait_recv()
        total = total + rs_recv[n].astype(F32)
    out_ref[...] = total.astype(BF16)

    for one in sent:
        one.wait_send()


def store_all(*refs):
    sources, targets, sem = refs[:4], refs[4:8], refs[8]
    stores = [pltpu.make_async_copy(sources[n], targets[n], sem.at[n]) for n in range(4)]
    for one in stores:
        one.start()
    for one in stores:
        one.wait()


def build(mesh, X):
    Y, Z = mesh.shape["seq"] // X, mesh.shape["head"] // 2
    rows = LENGTH // X
    dma = pltpu.SemaphoreType.DMA

    def block(*lead):
        return pltpu.VMEM((*lead, LENGTH, WIDTH), BF16)

    def wide(*lead):
        return pltpu.VMEM((*lead, LENGTH, WIDTH), F32)

    def message(n, count):
        return pltpu.VMEM((n, count, DH), BF16)

    def small_scratch():
        return [
            pltpu.VMEM((SMALL, DH), BF16),
            message(X, SMALL),
            pltpu.VMEM((SMALL, DH), BF16),
            message(Y, SMALL),
        ]

    most = max(X, Y)
    scratch = [
        pltpu.SMEM((2,), F32),
        block(),
        block(),
        block(),
        block(Z),
        pltpu.VMEM((Z, 2 * WIDTH, WIDTH), BF16),
        pltpu.VMEM((2, LENGTH, LENGTH), F32),
        wide(),
        block(),
        wide(),
        block(),
        block(),
        pltpu.VMEM((WIDTH, LENGTH), F32),
        pltpu.VMEM((WIDTH, LENGTH), F32),
        wide(Z),
        block(8),
        block(8),
        message(X, 2 * rows),
        message(X, 2 * rows),
        message(1, 2 * rows),
        message(Y, 2 * rows),
        pltpu.VMEM((X, rows, WIDTH), BF16),
        block(),
        message(X, 2 * rows),
        message(X, 2 * rows),
        message(1, 2 * rows),
        message(Y, 2 * rows),
        pltpu.VMEM((X, rows, WIDTH), BF16),
        block(),
        *small_scratch(),
        *small_scratch(),
        dma((5,)),
        dma((Z,)),
        dma((10, most)),
        dma((10, most)),
        dma((8,)),
        dma((8,)),
        dma((Z,)),
        dma((Z,)),
        dma((2,)),
        dma((2,)),
        dma((8,)),
        dma((8,)),
    ]

    def shards(queries, keys, values, gate, out_weight, out_grad, valid, starts):
        one = jax.ShapeDtypeStruct((LENGTH, WIDTH), BF16)
        results = pl.pallas_call(
            functools.partial(layer, (X, Y, Z)),
            out_shape=(one,) * 4,
            in_specs=[pl.BlockSpec(memory_space=pltpu.SMEM)] * 2
            + [pl.BlockSpec(memory_space=pltpu.HBM)] * 6,
            out_specs=(pl.BlockSpec(memory_space=pltpu.VMEM),) * 4,
            scratch_shapes=scratch,
            compiler_params=pltpu.CompilerParams(
                collective_id=0, has_side_effects=True, vmem_limit_bytes=32 * 1024 * 1024
            ),
            name="layer",
        )(
            valid,
            starts,
            *(
                pltpu.with_memory_space_constraint(a, pltpu.HBM)
                for a in (gate, queries, keys, values, out_grad, out_weight)
            ),
        )
        return pl.pallas_call(
            store_all,
            out_shape=(one,) * 4,
            in_specs=[pl.BlockSpec(memory_space=pltpu.VMEM)] * 4,
            out_specs=(pl.BlockSpec(memory_space=pltpu.HBM),) * 4,
            scratch_shapes=[dma((4,))],
            name="store_all",
        )(*(pltpu.with_memory_space_constraint(a, pltpu.VMEM) for a in results))

    placed = (
        P("seq", "head"),
        P("seq", "head"),
        P("seq", "head"),
        P("head"),
        P("head", None),
        P("seq", "head"),
        P("seq"),
        P("seq"),
    )
    return jax.shard_map(
        shards, mesh=mesh, in_specs=placed, out_specs=(P("seq", "head"),) * 4, check_vma=False
    )


def solution(mesh):
    return build(mesh, 8)
```

```python
import functools

import jax
import jax.numpy as jnp
from jax import lax
from jax.experimental import pallas as pl
from jax.experimental.pallas import tpu as pltpu
from jax.sharding import PartitionSpec as P

DH = 128
LENGTH = 128
WIDTH = 2 * DH
SMALL = 16
SCALE = DH ** (-0.5)
MESH = pl.DeviceIdType.MESH
F32, BF16 = jnp.float32, jnp.bfloat16


def dot(a, b, contract_a, contract_b):
    return lax.dot_general(
        a, b, (((contract_a,), (contract_b,)), ((), ())), preferred_element_type=F32
    )


def phi(x):
    return jnp.where(x > 0, x + 1.0, jnp.exp(jnp.minimum(x, 0.0)))


def phi_slope(x):
    return jnp.where(x > 0, 1.0, jnp.where(x == 0, 0.5, jnp.exp(jnp.minimum(x, 0.0))))


def both(one):
    return jnp.concatenate([one(slice(0, DH)), one(slice(DH, WIDTH))], axis=1)


def small_rows(norm, flag):
    high = norm.astype(BF16).astype(F32)
    low = norm - high
    at = lax.broadcasted_iota(jnp.int32, (SMALL, DH), 0)
    rows = jnp.zeros((SMALL, DH), F32)
    for n, row in enumerate(
        (high[:, :DH], high[:, DH:], low[:, :DH], low[:, DH:], flag[:, :DH])
    ):
        rows = jnp.where(at == n, row, rows)
    return rows.astype(BF16)


def split_small(small):
    small = small.astype(F32)
    norm = jnp.concatenate([small[0:1] + small[2:3], small[1:2] + small[3:4]], axis=1)
    return norm, jnp.concatenate([small[4:5], small[4:5]], axis=1)


def layer(
    sizes,
    valid_ref,
    starts_ref,
    gate_hbm,
    q_hbm,
    k_hbm,
    v_hbm,
    og_hbm,
    w_hbm,
    out_ref,
    dq_ref,
    dk_ref,
    dv_ref,
    gate_ref,
    q_ref,
    k_ref,
    v_ref,
    og_all,
    w_blocks,
    probs_ref,
    local_ref,
    sigq_ref,
    read_ref,
    mixed_ref,
    mixed_other,
    grad_theirs,
    grad_other,
    part_ref,
    rs_send,
    rs_recv,
    f_msg1,
    f_buf1,
    f_msg2,
    f_buf2,
    f_msg3,
    f_in,
    b_msg1,
    b_buf1,
    b_msg2,
    b_buf2,
    b_msg3,
    b_in,
    s_msg1,
    s_buf1,
    s_msg2,
    s_buf2,
    n_msg1,
    n_buf1,
    n_msg2,
    n_buf2,
    load_sem,
    own_sem,
    scan_send,
    scan_recv,
    ag_send,
    ag_recv,
    w_send,
    w_recv,
    swap_send,
    swap_recv,
    rs_send_sem,
    rs_recv_sem,
):
    X, Y, Z = sizes
    rows = LENGTH // X
    half = LENGTH // 2
    seq, head = lax.axis_index("seq"), lax.axis_index("head")
    y, x = lax.div(seq, X), lax.rem(seq, X)
    z, core = lax.div(head, 2), lax.rem(head, 2)

    def x_peer(j):
        return (y * X + lax.rem(x + j, X), head)

    def y_peer(j):
        return (lax.rem(y + j, Y) * X + x, head)

    def z_at(j):
        return lax.rem(z + j + Z, Z)

    def z_peer(j):
        return (seq, z_at(j) * 2 + core)

    partner = (seq, z * 2 + (1 - core))
    sent = []

    def remote(src, dst, send, recv, peer):
        one = pltpu.make_async_remote_copy(
            src_ref=src,
            dst_ref=dst,
            send_sem=send,
            recv_sem=recv,
            device_id=peer,
            device_id_type=MESH,
        )
        one.start()
        sent.append(one)
        return one

    loads = {}
    for n, (name, src, dst) in enumerate(
        (
            ("og", og_hbm, og_all.at[z]),
            ("k", k_hbm, k_ref),
            ("v", v_hbm, v_ref),
            ("gate", gate_hbm, gate_ref),
            ("q", q_hbm, q_ref),
        )
    ):
        loads[name] = pltpu.make_async_copy(src, dst, load_sem.at[n])
        loads[name].start()

    barrier = pltpu.get_barrier_semaphore()
    peers = [x_peer(j) for j in range(1, X)] + [y_peer(j) for j in range(1, Y)]
    relayed = Z == 8
    straight = (2, 6, 1, 7) if relayed else tuple(range(1, Z))
    peers += [z_peer(j) for j in straight] + [partner]
    for peer in peers:
        pl.semaphore_signal(barrier, inc=1, device_id=peer, device_id_type=MESH)

    def far_first(n):
        return sorted(range(1, n), key=lambda j: -min(j, n - j))

    def along_x(phase, source, target):
        return [
            remote(
                source(lax.rem(x + j, X)),
                target,
                scan_send.at[phase, j],
                scan_recv.at[phase, j],
                x_peer(j),
            )
            for j in far_first(X)
        ]

    def along_y(phase, source, target):
        return [
            remote(source, target, scan_send.at[phase, j], scan_recv.at[phase, j], y_peer(j))
            for j in far_first(Y)
        ]

    def arrived(copies):
        for one in copies:
            one.wait_recv()

    def pack(ref, place, block):
        ref[place, 0:rows, :] = block[:, :DH]
        ref[place, rows : 2 * rows, :] = block[:, DH:]

    def unpack(ref, place):
        return jnp.concatenate(
            [ref[place, 0:rows, :], ref[place, rows : 2 * rows, :]], axis=1
        ).astype(F32)

    zero_block, zero_row = jnp.zeros((rows, WIDTH), F32), jnp.zeros((1, WIDTH), F32)
    x_row, y_row = jnp.full((1, WIDTH), x, jnp.int32), jnp.full((1, WIDTH), y, jnp.int32)
    here = pl.ds(pl.multiple_of(x * rows, rows), rows)

    upper, lower, full = slice(0, half), slice(half, LENGTH), slice(0, LENGTH)

    def gather(n, block, part, to):
        piece = og_all.at[z_at(block), part]
        return remote(piece, piece, ag_send.at[n], ag_recv.at[n], z_peer(to))

    pl.semaphore_wait(barrier, len(peers))
    loads["og"].wait()
    gathers = {n: gather(n, 0, full, to) for n, to in enumerate(straight)}

    live = lax.broadcasted_iota(jnp.int32, (LENGTH, WIDTH), 0) < valid_ref[0]
    flag = jnp.full((1, WIDTH), starts_ref[0], jnp.int32).astype(F32)
    loads["k"].wait()
    sigk = jnp.where(live, phi(k_ref[...].astype(F32)), 0.0)
    s_msg1[...] = small_rows(jnp.sum(sigk, axis=0, keepdims=True), flag)
    s_buf1[x] = s_msg1[...]
    s_first = along_x(8, lambda to: s_msg1, s_buf1.at[x])
    sigk_low = sigk.astype(BF16)
    loads["v"].wait()
    state = both(lambda h: dot(sigk_low[:, h], v_ref[:, h], 0, 0)).astype(BF16)
    for i in range(X):
        pack(f_msg1, i, state[i * rows : (i + 1) * rows])
    f_buf1[x] = f_msg1[x]
    first = along_x(0, lambda to: f_msg1.at[to], f_buf1.at[x])

    weights, own_weights = [], []
    for i in range(Z):
        columns = pl.ds(pl.multiple_of((2 * i + 1 - core) * WIDTH, WIDTH), WIDTH)
        weights.append(
            remote(
                w_hbm.at[:, columns],
                w_blocks.at[i, WIDTH:, :],
                w_send.at[i],
                w_recv.at[i],
                partner,
            )
        )
    for i in range(Z):
        columns = pl.ds(pl.multiple_of((2 * i + core) * WIDTH, WIDTH), WIDTH)
        own_weights.append(
            pltpu.make_async_copy(w_hbm.at[:, columns], w_blocks.at[i, 0:WIDTH, :], own_sem.at[i])
        )
        own_weights[i].start()

    loads["gate"].wait()
    lanes = lax.broadcasted_iota(jnp.int32, (1, WIDTH), 1)
    logit = jnp.where(
        lanes < DH, jnp.full((1, WIDTH), gate_ref[0], F32), jnp.full((1, WIDTH), gate_ref[1], F32)
    )
    gate = 1.0 / (1.0 + jnp.exp(-logit))

    loads["q"].wait()
    row = lax.broadcasted_iota(jnp.int32, (LENGTH, LENGTH), 0)
    col = lax.broadcasted_iota(jnp.int32, (LENGTH, LENGTH), 1)
    allowed = (col <= row) & (col < valid_ref[0])

    def attend(n):
        h = slice(n * DH, (n + 1) * DH)
        scores = dot(q_ref[:, h], k_ref[:, h], 1, 1) * SCALE
        scores = jnp.where(allowed, scores, -1e30)
        expo = jnp.exp(scores - jnp.max(scores, axis=1, keepdims=True))
        probs = expo / jnp.sum(expo, axis=1, keepdims=True)
        probs_ref[n] = probs
        local_ref[:, h] = dot(probs.astype(BF16), v_ref[:, h], 1, 0)

    attend(0)
    if relayed:
        for n, (came, block, part, to) in enumerate(
            ((0, -2, upper, 2), (0, -2, full, 1), (1, 2, lower, -2), (1, 2, full, -1))
        ):
            if n % 2 == 0:
                gathers[came].wait_recv()
            gathers[4 + n] = gather(4 + n, block, part, to)

    arrived(s_first)
    row_small = [split_small(s_buf1[i]) for i in range(X)]
    opened = [1.0 - start for _, start in row_small]
    acc_norm, still_open = zero_row, jnp.ones((1, WIDTH), F32)
    for i in range(X):
        acc_norm = opened[i] * acc_norm + row_small[i][0]
        still_open = still_open * opened[i]
    s_msg2[...] = small_rows(acc_norm, still_open)
    s_buf2[y] = s_msg2[...]
    s_second = along_y(9, s_msg2, s_buf2.at[y])

    attend(1)

    arrived(first)
    acc = zero_block
    for i in range(X):
        acc = opened[i] * acc + unpack(f_buf1, i)
    pack(f_msg2, 0, acc.astype(BF16))
    f_buf2[y] = f_msg2[0]
    second = along_y(1, f_msg2.at[0], f_buf2.at[y])

    sigq = phi(q_ref[...].astype(F32))
    sigq_ref[...] = sigq.astype(BF16)

    def cotangent(j):
        block = z_at(j)
        return dot(w_blocks[block], og_all[block], 1, 1)

    for one in own_weights:
        one.wait()
    arrived(weights)
    grads = cotangent(0)
    steps = ((0, 2), (1, 6), (2, 1), (3, 7)) if relayed else enumerate(straight)
    for n, to in steps:
        if not relayed or n > 1:
            gathers[n].wait_recv()
        grads = grads + cotangent(-to)
    if relayed:
        for came, block in (((5,), -3), ((7,), 3), ((4, 6), 4)):
            for n in came:
                gathers[n].wait_recv()
            grads = grads + cotangent(block)
    mine = grads[:WIDTH]
    grad_theirs[...] = grads[WIDTH:]
    swap = remote(grad_theirs, grad_other, swap_send.at[0], swap_recv.at[0], partner)

    arrived(s_second)
    rows_small = [split_small(s_buf2[i]) for i in range(Y)]
    acc_norm, norm_in = zero_row, zero_row
    for i in range(Y):
        norm, still_open = rows_small[i]
        acc_norm = jnp.where(y_row > i, norm + still_open * acc_norm, acc_norm)
    for i in range(X):
        acc_norm = opened[i] * acc_norm
        norm_in = jnp.where(x_row == i, acc_norm, norm_in)
        acc_norm = acc_norm + row_small[i][0]
    scaled = sigq * norm_in
    inverse = both(
        lambda h: jnp.broadcast_to(
            1.0 / (jnp.sum(scaled[:, h], axis=1, keepdims=True) + 1.0), (LENGTH, DH)
        )
    )

    arrived(second)
    acc = zero_block
    for i in range(Y):
        acc = jnp.where(y_row > i, unpack(f_buf2, i) + rows_small[i][1] * acc, acc)
    for i in range(X):
        acc = opened[i] * acc
        f_msg3[i] = acc.astype(BF16)
        acc = acc + unpack(f_buf1, i)
    f_in[here, :] = f_msg3[x]
    third = along_x(2, lambda to: f_msg3.at[to], f_in.at[here, :])

    gated = jnp.where(live, gate * inverse, 0.0)
    mixed_local = jnp.where(live, (1.0 - gate) * local_ref[...], 0.0)

    swap.wait_recv()
    grad = jnp.where(live, (mine + grad_other[...]).T.astype(BF16).astype(F32), 0.0)
    read_grad = gate * grad
    local_grad = ((1.0 - gate) * grad).astype(BF16)
    numer_grad = (gated * grad).astype(BF16)
    state_grad = both(lambda h: dot(sigq_ref[:, h], numer_grad[:, h], 0, 0)).astype(BF16)
    for i in range(X):
        pack(b_msg1, i, state_grad[i * rows : (i + 1) * rows])
    b_buf1[x] = b_msg1[x]
    b_first = along_x(3, lambda to: b_msg1.at[to], b_buf1.at[x])

    arrived(third)
    numer = both(lambda h: dot(sigq_ref[:, h], f_in[:, h], 1, 0))
    mixed_ref[...] = (gated * numer + mixed_local).astype(BF16)
    mixing = remote(mixed_ref, mixed_other, swap_send.at[1], swap_recv.at[1], partner)

    product = read_grad * (numer * inverse)
    denom_grad = -inverse * both(
        lambda h: jnp.broadcast_to(jnp.sum(product[:, h], axis=1, keepdims=True), (LENGTH, DH))
    )
    n_msg1[...] = small_rows(jnp.sum(sigq * denom_grad, axis=0, keepdims=True), flag)
    n_buf1[x] = n_msg1[...]
    n_first = along_x(6, lambda to: n_msg1, n_buf1.at[x])

    early = len(sent)

    arrived(b_first)
    acc = zero_block
    for i in range(X - 1, -1, -1):
        acc = opened[i] * (acc + unpack(b_buf1, i))
    pack(b_msg2, 0, acc.astype(BF16))
    b_buf2[y] = b_msg2[0]
    b_second = along_y(4, b_msg2.at[0], b_buf2.at[y])

    reduce_order = [j for j in (4, 3, 5, 1, 7, 2, 6, 0) if relayed] or list(range(Z))
    for j in reduce_order[:3]:
        part_ref[j] = dot(mixed_ref[...], w_blocks[z_at(j), 0:WIDTH, :], 1, 0)

    mixing.wait_recv()
    reduces = {}

    def whole(j):
        j = j % Z
        block = z_at(j)
        if j in reduce_order[:3]:
            part = part_ref[j]
        else:
            part = dot(mixed_ref[...], w_blocks[block, 0:WIDTH, :], 1, 0)
        return part + dot(mixed_other[...], w_blocks[block, WIDTH:, :], 1, 0)

    def reduce(n, value, part, to):
        rs_send[n, part] = value.astype(BF16)
        reduces[n] = remote(
            rs_send.at[n, part],
            rs_recv.at[n, part],
            rs_send_sem.at[n],
            rs_recv_sem.at[n],
            z_peer(to),
        )

    if relayed:
        across = whole(4)
        reduce(4, across[upper], upper, 2)
        reduce(6, across[lower], lower, -2)
        reduce(5, whole(3), full, 1)
        reduce(7, whole(-3), full, -1)
        reduce(2, whole(1), full, 1)
        reduce(3, whole(-1), full, -1)
        part_ref[2] = whole(2)
        part_ref[6] = whole(6)
    else:
        for n, to in enumerate(straight):
            reduce(n, whole(to), full, to)
    part_ref[0] = whole(0)

    parts = []
    for n in range(2):
        h = slice(n * DH, (n + 1) * DH)
        probs = probs_ref[n]
        probs_grad = dot(local_grad[:, h], v_ref[:, h], 1, 1)
        inner = jnp.sum(probs_grad * probs, axis=1, keepdims=True)
        scores_grad = (probs * (probs_grad - inner) * SCALE).astype(BF16)
        parts.append(
            (
                dot(scores_grad, k_ref[:, h], 1, 0)
                + (dot(numer_grad[:, h], f_in[:, h], 1, 1) + denom_grad[:, h] * norm_in[:, h])
                * phi_slope(q_ref[:, h].astype(F32)),
                dot(scores_grad, q_ref[:, h], 0, 0),
                dot(probs.astype(BF16), local_grad[:, h], 0, 0),
            )
        )
    dq_ref[...] = jnp.concatenate([parts[0][0], parts[1][0]], axis=1).astype(BF16)
    key_part = jnp.concatenate([parts[0][1], parts[1][1]], axis=1)
    value_part = jnp.concatenate([parts[0][2], parts[1][2]], axis=1)

    arrived(n_first)
    acc_norm = zero_row
    for i in range(X - 1, -1, -1):
        acc_norm = opened[i] * (acc_norm + split_small(n_buf1[i])[0])
    n_msg2[...] = small_rows(acc_norm, flag)
    n_buf2[y] = n_msg2[...]
    n_second = along_y(7, n_msg2, n_buf2.at[y])

    if relayed:
        for n, straight_on, across, part, to in ((0, 5, 4, upper, 2), (1, 7, 6, lower, -2)):
            reduces[straight_on].wait_recv()
            reduces[across].wait_recv()
            j = to % Z
            part_ref[j] = part_ref[j] + rs_recv[straight_on].astype(F32)
            part_ref[j, part] = part_ref[j, part] + rs_recv[across, part].astype(F32)
            reduce(n, part_ref[j], full, to)

    arrived(b_second)
    acc = zero_block
    for i in range(Y - 1, -1, -1):
        acc = jnp.where(y_row < i, unpack(b_buf2, i) + rows_small[i][1] * acc, acc)
    for i in range(X - 1, -1, -1):
        b_msg3[i] = acc.astype(BF16)
        acc = opened[i] * (acc + unpack(b_buf1, i))
    b_in[here, :] = b_msg3[x]
    b_third = along_x(5, lambda to: b_msg3.at[to], b_in.at[here, :])

    arrived(n_second)
    acc_norm = zero_row
    for i in range(Y - 1, -1, -1):
        acc_norm = jnp.where(
            y_row < i, split_small(n_buf2[i])[0] + rows_small[i][1] * acc_norm, acc_norm
        )
    norm_back = zero_row
    for i in range(X - 1, -1, -1):
        norm_back = jnp.where(x_row == i, acc_norm, norm_back)
        acc_norm = opened[i] * (acc_norm + split_small(n_buf1[i])[0])

    k_float = k_ref[...].astype(F32)
    slope = jnp.where(live, phi_slope(k_float), 0.0)
    sigk_low = jnp.where(live, phi(k_float), 0.0).astype(BF16)
    key_part = key_part + norm_back * slope
    for one in sent[:early]:
        one.wait_send()
    arrived(b_third)
    key_more = both(lambda h: dot(v_ref[:, h], b_in[:, h], 1, 1)) * slope
    dk_ref[...] = (key_part + key_more).astype(BF16)
    value_more = both(lambda h: dot(sigk_low[:, h], b_in[:, h], 1, 0))
    dv_ref[...] = (value_part + value_more).astype(BF16)

    total = part_ref[0]
    for n in (2, 3, 0, 1) if relayed else range(Z - 1):
        reduces[n].wait_recv()
        total = total + rs_recv[n].astype(F32)
    out_ref[...] = total.astype(BF16)

    for one in sent[early:]:
        one.wait_send()


def store_all(*refs):
    sources, targets, sem = refs[:4], refs[4:8], refs[8]
    stores = [pltpu.make_async_copy(sources[n], targets[n], sem.at[n]) for n in range(4)]
    for one in stores:
        one.start()
    for one in stores:
        one.wait()


def build(mesh, X):
    Y, Z = mesh.shape["seq"] // X, mesh.shape["head"] // 2
    rows = LENGTH // X
    dma = pltpu.SemaphoreType.DMA

    def block(*lead):
        return pltpu.VMEM((*lead, LENGTH, WIDTH), BF16)

    def wide(*lead):
        return pltpu.VMEM((*lead, LENGTH, WIDTH), F32)

    def message(n, count):
        return pltpu.VMEM((n, count, DH), BF16)

    def small_scratch():
        return [
            pltpu.VMEM((SMALL, DH), BF16),
            message(X, SMALL),
            pltpu.VMEM((SMALL, DH), BF16),
            message(Y, SMALL),
        ]

    most = max(X, Y)
    scratch = [
        pltpu.SMEM((2,), F32),
        block(),
        block(),
        block(),
        block(Z),
        pltpu.VMEM((Z, 2 * WIDTH, WIDTH), BF16),
        pltpu.VMEM((2, LENGTH, LENGTH), F32),
        wide(),
        block(),
        wide(),
        block(),
        block(),
        pltpu.VMEM((WIDTH, LENGTH), F32),
        pltpu.VMEM((WIDTH, LENGTH), F32),
        wide(Z),
        block(8),
        block(8),
        message(X, 2 * rows),
        message(X, 2 * rows),
        message(1, 2 * rows),
        message(Y, 2 * rows),
        pltpu.VMEM((X, rows, WIDTH), BF16),
        block(),
        message(X, 2 * rows),
        message(X, 2 * rows),
        message(1, 2 * rows),
        message(Y, 2 * rows),
        pltpu.VMEM((X, rows, WIDTH), BF16),
        block(),
        *small_scratch(),
        *small_scratch(),
        dma((5,)),
        dma((Z,)),
        dma((10, most)),
        dma((10, most)),
        dma((8,)),
        dma((8,)),
        dma((Z,)),
        dma((Z,)),
        dma((2,)),
        dma((2,)),
        dma((8,)),
        dma((8,)),
    ]

    def shards(queries, keys, values, gate, out_weight, out_grad, valid, starts):
        one = jax.ShapeDtypeStruct((LENGTH, WIDTH), BF16)
        results = pl.pallas_call(
            functools.partial(layer, (X, Y, Z)),
            out_shape=(one,) * 4,
            in_specs=[pl.BlockSpec(memory_space=pltpu.SMEM)] * 2
            + [pl.BlockSpec(memory_space=pltpu.HBM)] * 6,
            out_specs=(pl.BlockSpec(memory_space=pltpu.VMEM),) * 4,
            scratch_shapes=scratch,
            compiler_params=pltpu.CompilerParams(
                collective_id=0, has_side_effects=True, vmem_limit_bytes=32 * 1024 * 1024
            ),
            name="layer",
        )(
            valid,
            starts,
            *(
                pltpu.with_memory_space_constraint(a, pltpu.HBM)
                for a in (gate, queries, keys, values, out_grad, out_weight)
            ),
        )
        return pl.pallas_call(
            store_all,
            out_shape=(one,) * 4,
            in_specs=[pl.BlockSpec(memory_space=pltpu.VMEM)] * 4,
            out_specs=(pl.BlockSpec(memory_space=pltpu.HBM),) * 4,
            scratch_shapes=[dma((4,))],
            name="store_all",
        )(*(pltpu.with_memory_space_constraint(a, pltpu.VMEM) for a in results))

    placed = (
        P("seq", "head"),
        P("seq", "head"),
        P("seq", "head"),
        P("head"),
        P("head", None),
        P("seq", "head"),
        P("seq"),
        P("seq"),
    )
    return jax.shard_map(
        shards, mesh=mesh, in_specs=placed, out_specs=(P("seq", "head"),) * 4, check_vma=False
    )


def solution(mesh):
    return build(mesh, 8)
```
